256 devices in a mesh: obs: 64 (over x, z, core), tile: 4 (over y).
Axes of the slice: x: 4, y: 4, z: 8, core: 2. Of those that a mesh axis runs over, the one named last changes fastest.
Arguments:
- jacobian: bfloat16 [16384, 65536], P(('obs', 'tile')), may hold values from -0.1875 to 0.1875
- obs_weight: float32 [16384], P(('obs', 'tile')), may hold values from 0.1 to 10
- block_order: int32 [512], replicated, may hold values from 0 to 511, each once
- tile_pairs: int32 [64, 64, 2], P('obs'), may hold values from 0 to 7, as said below
- tile_count: int32 [64], P('obs'), may hold values from 1 to 64, as said below
Outputs:
- hessian: float32 [4096, 128, 128], P(('obs', 'tile'))
The draws below stay inside these ranges and needn't reach their ends.
Inputs may be any that keep to these rules, and one draw needn't show every extreme that they name: `tile_pairs`: slot numbers within an owner's own 8 slots; the first tile_count[j] pairs of owner j are distinct. `tile_count`: some owner has 64 live tiles.
All inputs are finite; a program needn't handle non-finite values.
Results may differ from the reference program's by a relative error of at most 0.0015.
Values may be sent and summed in bfloat16 or wider, within the bound.
No kernel may reach another device: no remote copies, remote signals or barrier semaphores. Data moves between devices by JAX's collectives and lax.ppermute only.
A program may use at most 256 MiB of HBM per device.

```python
import math
import jax
import jax.numpy as jnp
from jax import lax

ZONES = 65536
BLOCK = 128
TILE_MAX = 64
OBS_ROWS = 16384
ZBLOCKS = 512
OWNERS = 64
ZB_DEV = 8


def draw_tile_count(key, part):
    first_key, second_key = jax.random.split(jax.random.fold_in(key, 11))
    counts = jax.random.randint(first_key, (OWNERS,), max(1, TILE_MAX // 8), TILE_MAX // 2 + 1, dtype=jnp.int32)
    busiest = jax.random.randint(second_key, (), 0, OWNERS, dtype=jnp.int32)
    return jnp.where(jnp.arange(OWNERS, dtype=jnp.int32) == busiest, TILE_MAX, counts).astype(jnp.int32)


def pick_pairs(owner_key):
    return jax.random.permutation(owner_key, ZB_DEV * ZB_DEV)[:TILE_MAX]


def draw_tile_pairs(key, part):
    owner_keys = jax.random.split(jax.random.fold_in(key, 23), OWNERS)
    orders = jax.vmap(pick_pairs)(owner_keys).astype(jnp.int32)
    return jnp.stack([orders // ZB_DEV, orders % ZB_DEV], axis=-1).astype(jnp.int32)


def levels(rng, dims, pieces, smallest, high):
    gain, own = 1.0, jax.random.fold_in(rng, 6)
    for position, shards_of in pieces:
        steps = jnp.exp(jax.random.uniform(jax.random.fold_in(own, position), (shards_of,), jnp.float32, smallest / len(pieces), high / len(pieces)))
        gain = gain * jnp.repeat(steps, dims[position] // shards_of).reshape([-1 if axis == position else 1 for axis in range(len(dims))])
    return gain


def centred(key, shape, scale, bound, cuts=(), held_as=jnp.bfloat16):
    gain = levels(key, shape, cuts, -0.22, 0.18) if cuts else 1.0
    entries = jax.random.normal(key, shape, jnp.float32) * scale * gain
    return jnp.minimum(jnp.maximum(entries, -bound), bound).astype(held_as)


def setup_inputs(seed: int = 0) -> dict:
    arg_keys = jax.random.split(jax.random.key(seed), 6)
    jacobian = centred(arg_keys[0], (OBS_ROWS, ZONES), (OBS_ROWS // 16) ** -0.5, 0.1875, ((0, 256),))
    obs_weight = jnp.clip(jnp.exp(math.log(10.0) - 4.6051702 * jax.random.uniform(arg_keys[1], (OBS_ROWS,), jnp.float32) ** levels(arg_keys[1], (OBS_ROWS,), ((0, 256),), -0.2, 0.2)), 0.1, 10.0)
    block_order = jax.random.permutation(arg_keys[2], ZBLOCKS).astype(jnp.int32)
    tile_pairs = draw_tile_pairs(jax.random.fold_in(arg_keys[5], 71), 0)
    tile_count = draw_tile_count(jax.random.fold_in(arg_keys[5], 71), 0)
    return dict(jacobian=jacobian, obs_weight=obs_weight, block_order=block_order, tile_pairs=tile_pairs, tile_count=tile_count)


def reference(jacobian, obs_weight, block_order, tile_pairs, tile_count):
    root_weight = jnp.sqrt(obs_weight)[:, None]

    def column_block(slot_index):
        zone_block = block_order[slot_index]
        column_piece = lax.dynamic_slice_in_dim(jacobian, (zone_block * BLOCK).astype(jnp.int32), BLOCK, 1)
        return (column_piece.astype(jnp.float32) * root_weight).astype(jnp.bfloat16)

    def owner_tiles(owner_index):

        def one_tile(tile_index):

            def compute(unused):
                left_block = column_block(owner_index * ZB_DEV + tile_pairs[owner_index, tile_index, 0])
                right_block = column_block(owner_index * ZB_DEV + tile_pairs[owner_index, tile_index, 1])
                return lax.dot_general(left_block, right_block, (((0,), (0,)), ((), ())), preferred_element_type=jnp.float32)

            def empty_tile(unused):
                return jnp.zeros((BLOCK, BLOCK), jnp.float32)
            return lax.cond(tile_index < tile_count[owner_index], compute, empty_tile, 0)
        return lax.map(one_tile, jnp.arange(TILE_MAX, dtype=jnp.int32))
    tiles = lax.map(owner_tiles, jnp.arange(OWNERS, dtype=jnp.int32))
    return tiles.reshape(OWNERS * TILE_MAX, BLOCK, BLOCK)
```

```python
import jax
import jax.numpy as jnp
from jax import lax
from jax.experimental import pallas as pl
from jax.experimental.pallas import tpu as pltpu
from jax.sharding import PartitionSpec as P

BLOCK = 128
ROW_STEP = 16


def scale_columns(owners, order, jacobian, weight):
    units = owners.shape[0]
    rows, zones = jacobian.shape
    own_blocks = 8
    width = own_blocks * BLOCK

    def kernel(owners_ref, order_ref, jac_ref, weight_ref, out_ref):
        root = jnp.sqrt(weight_ref[...])

        def unit(u, carry):
            base = owners_ref[u] * own_blocks
            for b in range(own_blocks):
                start = pl.multiple_of(order_ref[base + b] * BLOCK, BLOCK)
                piece = jac_ref[:, pl.ds(start, BLOCK)].astype(jnp.float32) * root
                out_ref[u, :, b * BLOCK : (b + 1) * BLOCK] = piece.astype(jnp.bfloat16)
            return carry

        lax.fori_loop(0, units, unit, 0)

    return pl.pallas_call(
        kernel,
        out_shape=jax.ShapeDtypeStruct((units, rows, width), jnp.bfloat16),
        grid_spec=pltpu.PrefetchScalarGridSpec(
            num_scalar_prefetch=2,
            grid=(rows // ROW_STEP,),
            in_specs=[
                pl.BlockSpec((ROW_STEP, zones), lambda i, *_: (i, 0)),
                pl.BlockSpec((ROW_STEP, BLOCK), lambda i, *_: (i, 0)),
            ],
            out_specs=pl.BlockSpec((units, ROW_STEP, width), lambda i, *_: (0, i, 0)),
        ),
        compiler_params=pltpu.CompilerParams(vmem_limit_bytes=40 << 20),
        cost_estimate=pl.CostEstimate(
            flops=units * rows * width, bytes_accessed=2 * (rows * zones + units * rows * width), transcendentals=0
        ),
        name="scale_columns",
    )(owners, order, jacobian, weight)


def gram_tiles(pieces, step, pairs, count):
    rows, width = pieces[0].shape
    slots = pairs.shape[0] // 2
    steps = rows // step
    strip = 256

    def kernel(pairs_ref, count_ref, *refs):
        piece_refs, out_ref, gram = refs[:-2], refs[-2], refs[-1]
        first = pl.program_id(0) == 0

        @pl.when(first)
        def _():
            gram[...] = jnp.zeros_like(gram)

        for ref in piece_refs:
            for m in range(0, width, strip):
                gram[m : m + strip, :] += lax.dot_general(
                    ref[:, m : m + strip], ref[...], (((0,), (0,)), ((), ())), preferred_element_type=jnp.float32
                )

        @pl.when(pl.program_id(0) == steps - 1)
        def _():
            def pick(k, carry):
                row = pl.multiple_of(pairs_ref[2 * k] * BLOCK, BLOCK)
                col = pl.multiple_of(pairs_ref[2 * k + 1] * BLOCK, BLOCK)
                tile = gram[pl.ds(row, BLOCK), pl.ds(col, BLOCK)]
                out_ref[k] = jnp.where(k < count_ref[0], tile, 0.0)
                return carry

            lax.fori_loop(0, slots, pick, 0)

    return pl.pallas_call(
        kernel,
        out_shape=jax.ShapeDtypeStruct((slots, BLOCK, BLOCK), jnp.float32),
        grid_spec=pltpu.PrefetchScalarGridSpec(
            num_scalar_prefetch=2,
            grid=(steps,),
            in_specs=[pl.BlockSpec((step, width), lambda i, *_: (i, 0)) for _ in pieces],
            out_specs=pl.BlockSpec((slots, BLOCK, BLOCK), lambda i, *_: (0, 0, 0)),
            scratch_shapes=[pltpu.VMEM((width, width), jnp.float32)],
        ),
        compiler_params=pltpu.CompilerParams(vmem_limit_bytes=40 << 20),
        cost_estimate=pl.CostEstimate(
            flops=2 * len(pieces) * rows * width * width,
            bytes_accessed=2 * len(pieces) * rows * width + 4 * slots * BLOCK * BLOCK,
            transcendentals=0,
        ),
        name="gram_tiles",
    )(pairs, count, *pieces)


def body(jacobian, obs_weight, block_order, tile_pairs, tile_count):
    rows = jacobian.shape[0]
    owners = lax.axis_size("obs")
    weight = jnp.broadcast_to(obs_weight[:, None], (rows, BLOCK))
    outgoing = scale_columns(jnp.arange(owners, dtype=jnp.int32), block_order, jacobian, weight)
    arrived = lax.all_to_all(outgoing, "obs", split_axis=0, concat_axis=0, tiled=True)
    columns = arrived.reshape(owners * rows, arrived.shape[2])
    tiles = gram_tiles([columns], 512, tile_pairs.reshape(-1), tile_count)
    return lax.psum_scatter(tiles, "tile", scatter_dimension=0, tiled=True)


def solution(mesh):
    return jax.shard_map(
        body,
        mesh=mesh,
        in_specs=(
            P(("obs", "tile"), None),
            P(("obs", "tile")),
            P(),
            P("obs", None, None),
            P("obs"),
        ),
        out_specs=P(("obs", "tile"), None, None),
        check_vma=False,
    )
```

```python
import jax
import jax.numpy as jnp
import numpy as np
from jax import lax
from jax.experimental import pallas as pl
from jax.experimental.pallas import tpu as pltpu
from jax.sharding import PartitionSpec as P

BLOCK = 128
OWN_BLOCKS = 8
WIDTH = OWN_BLOCKS * BLOCK
ROW_STEP = 16
FAR = 3
BOTH_STEPS = (0, 1, -1)
FAR_STEP = -2
NEAR_STEP = 2
NEAR_AHEAD = 6
VMEM = 62 << 20
CODES = 32000.0
HBM = pl.BlockSpec(memory_space=pltpu.HBM)


def scale_columns(owners, order, jacobian, weight, sizes):
    units = sum(sizes)
    firsts = np.cumsum([0, *sizes])
    rows, zones = jacobian.shape
    groups = rows // ROW_STEP
    batch = 8

    def kernel(owners_ref, order_ref, jac_ref, weight_ref, *refs):
        out_refs, (held, made, in_sems, out_sems) = refs[:-4], refs[-4:]
        cut = zones // 4

        def load(g, q):
            place = (pl.ds(g * ROW_STEP, ROW_STEP), pl.ds(q * cut, cut))
            return pltpu.make_async_copy(jac_ref.at[place], held.at[place], in_sems.at[g, q])

        def store(q):
            unit = made.at[pl.ds(int(firsts[q]), sizes[q])]
            return pltpu.make_async_copy(unit, out_refs[q], out_sems.at[q])

        for g in range(groups):
            for q in range(4):
                load(g, q).start()
        stored = 0
        for g in range(groups):
            for q in range(4):
                load(g, q).wait()
            span = pl.ds(g * ROW_STEP, ROW_STEP)
            root = jnp.sqrt(weight_ref[span, :])

            def unit(u, carry, span=span, root=root):
                base = owners_ref[u] * OWN_BLOCKS
                for b in range(OWN_BLOCKS):
                    start = pl.multiple_of(order_ref[base + b] * BLOCK, BLOCK)
                    piece = held[span, pl.ds(start, BLOCK)].astype(jnp.float32) * root
                    made[u, span, b * BLOCK : (b + 1) * BLOCK] = piece.astype(jnp.bfloat16)
                return carry

            if g < groups - 1:
                lax.fori_loop(0, units, unit, 0)
            else:
                for first in range(0, units, batch):
                    lax.fori_loop(first, first + batch, unit, 0)
                    while stored < len(sizes) and firsts[stored + 1] <= first + batch:
                        store(stored).start()
                        stored += 1
        for q in range(len(sizes)):
            store(q).wait()

    return pl.pallas_call(
        kernel,
        out_shape=[jax.ShapeDtypeStruct((size, rows, WIDTH), jnp.bfloat16) for size in sizes],
        grid_spec=pltpu.PrefetchScalarGridSpec(
            num_scalar_prefetch=2,
            grid=(),
            in_specs=[HBM, pl.BlockSpec(memory_space=pltpu.VMEM)],
            out_specs=[HBM] * len(sizes),
            scratch_shapes=[
                pltpu.VMEM((rows, zones), jnp.bfloat16),
                pltpu.VMEM((units, rows, WIDTH), jnp.bfloat16),
                pltpu.SemaphoreType.DMA((groups, 4)),
                pltpu.SemaphoreType.DMA((len(sizes),)),
            ],
        ),
        compiler_params=pltpu.CompilerParams(vmem_limit_bytes=VMEM),
        cost_estimate=pl.CostEstimate(
            flops=units * rows * WIDTH, bytes_accessed=2 * (rows * zones + units * rows * WIDTH), transcendentals=0
        ),
        name="scale_columns",
    )(owners, order, jacobian, weight)


def code_tile(tile):
    top = jnp.maximum(jnp.max(jnp.abs(tile), axis=0, keepdims=True), 1e-30)
    power = jnp.floor(jnp.log2(top)) + 1.0
    codes = jnp.round(tile * (jnp.exp2(-power) * CODES)).astype(jnp.int32).astype(jnp.int16)
    return codes, power


def decode_tile(codes, power):
    return codes.astype(jnp.int32).astype(jnp.float32) * (jnp.exp2(power) * (1.0 / CODES))


def gram_tiles(pieces, parts, pairs, count):
    rows, width = pieces[0].shape[1:]
    total = len(pieces) * rows
    slots = pairs.shape[0] // 2
    quarter = slots // 4
    strip, deep = 256, 512
    per = deep // rows

    def kernel(pairs_ref, count_ref, *refs):
        piece_refs, (out_ref, held, gram, made, powers, sems, out_sems) = refs[:-7], refs[-7:]

        def store(t):
            return pltpu.make_async_copy(made.at[t], out_ref.at[t], out_sems.at[t])

        def load(p):
            return pltpu.make_async_copy(piece_refs[p].at[parts[p]], held.at[pl.ds(p * rows, rows)], sems.at[p])

        for p in range(len(pieces)):
            load(p).start()
        for first in range(0, len(pieces), per):
            for p in range(first, first + per):
                load(p).wait()
            span = pl.ds(first * rows, deep)

            def multiply(m, carry, first=first, span=span):
                lanes = pl.ds(pl.multiple_of(m * strip, strip), strip)
                part = lax.dot_general(
                    held[span, lanes], held[span, :], (((0,), (0,)), ((), ())), preferred_element_type=jnp.float32
                )
                if first == 0:
                    gram[lanes, :] = part
                else:
                    gram[lanes, :] += part
                return carry

            lax.fori_loop(0, width // strip, multiply, 0)

        for t in range(4):

            def pick(k, carry, t=t):
                slot = t * quarter + k
                row = pl.multiple_of(pairs_ref[2 * slot] * BLOCK, BLOCK)
                col = pl.multiple_of(pairs_ref[2 * slot + 1] * BLOCK, BLOCK)
                tile = gram[pl.ds(row, BLOCK), pl.ds(col, BLOCK)]
                tile = jnp.where(slot < count_ref[0], tile, 0.0)
                codes, power = code_tile(tile)
                made[t, pl.ds(pl.multiple_of(k * BLOCK, BLOCK), BLOCK), :] = codes
                powers[pl.ds(k, 1), :] = power
                return carry

            lax.fori_loop(0, quarter, pick, 0)
            made[t, quarter * BLOCK :, :] = powers[...].astype(jnp.int32).astype(jnp.int16)
            store(t).start()
        for t in range(4):
            store(t).wait()

    return pl.pallas_call(
        kernel,
        out_shape=jax.ShapeDtypeStruct((4, quarter * BLOCK + quarter, BLOCK), jnp.int16),
        grid_spec=pltpu.PrefetchScalarGridSpec(
            num_scalar_prefetch=2,
            grid=(),
            in_specs=[HBM] * len(pieces),
            out_specs=HBM,
            scratch_shapes=[
                pltpu.VMEM((total, width), jnp.bfloat16),
                pltpu.VMEM((width, width), jnp.float32),
                pltpu.VMEM((4, quarter * BLOCK + quarter, BLOCK), jnp.int16),
                pltpu.VMEM((quarter, BLOCK), jnp.float32),
                pltpu.SemaphoreType.DMA((len(pieces),)),
                pltpu.SemaphoreType.DMA((4,)),
            ],
        ),
        compiler_params=pltpu.CompilerParams(vmem_limit_bytes=VMEM),
        cost_estimate=pl.CostEstimate(
            flops=2 * total * width * width, bytes_accessed=2 * total * width + 2 * slots * BLOCK * BLOCK,
            transcendentals=0,
        ),
        name="gram_tiles",
    )(pairs, count, *pieces)


def sum_tiles(parts, coded):
    rows = parts[0].shape[1]
    tiles = rows // (BLOCK + 1)
    sources = sum(p.shape[0] for p in parts)

    def kernel(*refs):
        part_refs, out_ref, powers = refs[: len(parts)], refs[len(parts)], refs[len(parts) + 1]
        scales, at = [], 0
        for ref in part_refs:
            for q in range(ref.shape[0]):
                powers[pl.ds(at * tiles, tiles), :] = ref[q, tiles * BLOCK :, :].astype(jnp.int32).astype(jnp.float32)
                at += 1

        def one(k, carry):
            span = pl.ds(pl.multiple_of(k * BLOCK, BLOCK), BLOCK)
            total, at = None, 0
            for ref in part_refs:
                for q in range(ref.shape[0]):
                    term = decode_tile(ref[q, span, :], powers[pl.ds(at * tiles + k, 1), :])
                    total = term if total is None else total + term
                    at += 1
            if coded:
                codes, power = code_tile(total)
                out_ref[0, span, :] = codes
                powers[pl.ds(sources * tiles + k, 1), :] = power
            else:
                out_ref[k] = total
            return carry

        lax.fori_loop(0, tiles, one, 0)
        if coded:
            own = powers[pl.ds(sources * tiles, tiles), :]
            out_ref[0, tiles * BLOCK :, :] = own.astype(jnp.int32).astype(jnp.int16)

    if coded:
        out = jax.ShapeDtypeStruct((1, rows, BLOCK), jnp.int16)
    else:
        out = jax.ShapeDtypeStruct((tiles, BLOCK, BLOCK), jnp.float32)
    vmem = pl.BlockSpec(memory_space=pltpu.VMEM)
    return pl.pallas_call(
        kernel,
        out_shape=out,
        in_specs=[vmem] * len(parts),
        out_specs=vmem,
        scratch_shapes=[pltpu.VMEM(((sources + 1) * tiles, BLOCK), jnp.float32)],
        compiler_params=pltpu.CompilerParams(vmem_limit_bytes=VMEM),
        cost_estimate=pl.CostEstimate(
            flops=4 * sources * rows * BLOCK, bytes_accessed=2 * (sources + 2) * rows * BLOCK, transcendentals=0
        ),
        name="sum_tiles",
    )(*parts)


def body(jacobian, obs_weight, block_order, tile_pairs, tile_count):
    rows = jacobian.shape[0]
    planes, lines, cores = lax.axis_size("z"), lax.axis_size("x"), lax.axis_size("c")
    x, z, c = lax.axis_index("x"), lax.axis_index("z"), lax.axis_index("c")
    weight = jnp.broadcast_to(obs_weight[:, None], (rows, BLOCK))
    places = [(dx, dc) for dx in range(lines) for dc in range(cores)]

    routes = [(dx, dc, s) for s in BOTH_STEPS for dx, dc in places]
    units = [(dx, dc, s, far) for dx, dc, s in routes for far in (0, 1)]
    sizes = [2] * len(routes)
    for far, s in ((1, FAR_STEP), (0, NEAR_STEP)):
        routes += [(dx, dc, s) for dx, dc in places]
        units += [(dx, dc, s, far) for dx, dc in places]
        sizes += [1] * len(places)
    table = np.array(units, np.int32)
    dest_c = c ^ table[:, 1]
    sign = 1 - 2 * dest_c
    dest_z = z + sign * (table[:, 2] - FAR * table[:, 3]) + planes
    owners = ((x + table[:, 0]) % lines * planes + dest_z % planes) * cores + dest_c

    def moved(value, dx, dc, s):
        if (dx, dc, s) == (0, 0, 0):
            return value
        moves = []
        for a in range(lines):
            for b in range(planes):
                for k in range(cores):
                    to_c = k ^ dc
                    to_z = (b + s * (1 - 2 * to_c)) % planes
                    moves.append(((a * planes + b) * cores + k, ((a + dx) % lines * planes + to_z) * cores + to_c))
        return lax.ppermute(value, ("x", "z", "c"), moves)

    wanted = jnp.concatenate([tile_pairs.reshape(-1), tile_count])
    far_wanted = moved(wanted, 0, 0, FAR)

    parts = scale_columns(owners.astype(jnp.int32), block_order, jacobian, weight, sizes)
    arrived = [moved(part, *route) for part, route in zip(parts, routes)]
    both = len(BOTH_STEPS) * len(places)
    shared, far_only, near_only = arrived[:both], arrived[both : both + len(places)], arrived[both + len(places) :]

    def swapped(pieces, index, table):
        index = [index] * len(shared) + [0] * len(places)
        tiles = gram_tiles(pieces, index, table[:-1], table[-1:])
        return lax.all_to_all(tiles, "y", split_axis=0, concat_axis=0, tiled=True)

    held_back = lax.optimization_barrier((far_only[0], *near_only[:NEAR_AHEAD]))
    far_only, near_only = [held_back[0], *far_only[1:]], [*held_back[1:], *near_only[NEAR_AHEAD:]]
    far = sum_tiles([swapped(shared + far_only, 1, far_wanted)], True)
    near = swapped(shared + near_only, 0, wanted)
    return sum_tiles([near, moved(far, 0, 0, -FAR)], False)


def solution(mesh):
    shape = (4, mesh.shape["obs"] // 8, 2, mesh.shape["tile"])
    chips = jax.sharding.Mesh(mesh.devices.reshape(shape), ("x", "z", "c", "y"))
    everywhere = ("x", "z", "c", "y")
    owner = ("x", "z", "c")
    return jax.shard_map(
        body,
        mesh=chips,
        in_specs=(P(everywhere, None), P(everywhere), P(), P(owner, None, None), P(owner)),
        out_specs=P(everywhere, None, None),
        check_vma=False,
    )
```

```python
import jax
import jax.numpy as jnp
import numpy as np
from jax import lax
from jax.experimental import pallas as pl
from jax.experimental.pallas import tpu as pltpu
from jax.sharding import PartitionSpec as P

BLOCK = 128
OWN_BLOCKS = 8
WIDTH = OWN_BLOCKS * BLOCK
FAR = 3
FAR_STEPS = (-2, -1, 1, 0)
CODES = 32000.0
VMEM = 62 << 20
HBM = pl.BlockSpec(memory_space=pltpu.HBM)


def scale_columns(owners, order, jacobian, weight, shapes):
    sizes = [int(np.prod(shape)) for shape in shapes]
    units = sum(sizes)
    firsts = np.cumsum([0, *sizes])
    rows, zones = jacobian.shape
    cuts, batch = 8, 4

    def kernel(owners_ref, order_ref, jac_ref, weight_ref, *refs):
        out_refs, (held, made, in_sems, out_sems) = refs[:-4], refs[-4:]
        cut = rows // cuts

        def load(q):
            span = pl.ds(q * cut, cut)
            return pltpu.make_async_copy(jac_ref.at[span], held.at[span], in_sems.at[q])

        def store(q):
            unit = made.at[pl.ds(int(firsts[q]), sizes[q])]
            return pltpu.make_async_copy(unit, out_refs[q], out_sems.at[q])

        for q in range(cuts):
            load(q).start()
        for q in range(cuts):
            load(q).wait()
        root = jnp.sqrt(weight_ref[...])

        def unit(u, carry):
            base = owners_ref[u] * OWN_BLOCKS
            for b in range(OWN_BLOCKS):
                start = pl.multiple_of(order_ref[base + b] * BLOCK, BLOCK)
                piece = held[:, pl.ds(start, BLOCK)].astype(jnp.float32) * root
                made[u, :, b * BLOCK : (b + 1) * BLOCK] = piece.astype(jnp.bfloat16)
            return carry

        for q in range(len(sizes)):
            lax.fori_loop(int(firsts[q]), int(firsts[q + 1]), unit, 0)
            store(q).start()
        for q in range(len(sizes)):
            store(q).wait()

    flat = pl.pallas_call(
        kernel,
        out_shape=[jax.ShapeDtypeStruct((size, rows, WIDTH), jnp.bfloat16) for size in sizes],
        grid_spec=pltpu.PrefetchScalarGridSpec(
            num_scalar_prefetch=2,
            grid=(),
            in_specs=[HBM, pl.BlockSpec(memory_space=pltpu.VMEM)],
            out_specs=[HBM] * len(sizes),
            scratch_shapes=[
                pltpu.VMEM((rows, zones), jnp.bfloat16),
                pltpu.VMEM((units, rows, WIDTH), jnp.bfloat16),
                pltpu.SemaphoreType.DMA((cuts,)),
                pltpu.SemaphoreType.DMA((len(sizes),)),
            ],
        ),
        compiler_params=pltpu.CompilerParams(vmem_limit_bytes=VMEM),
        cost_estimate=pl.CostEstimate(
            flops=units * rows * WIDTH, bytes_accessed=2 * (rows * zones + units * rows * WIDTH), transcendentals=0
        ),
        name="scale_columns",
    )(owners, order, jacobian, weight)
    return [part.reshape(*shape, rows, WIDTH) for part, shape in zip(flat, shapes)]


def copy_parts(arrays, shapes, copies, name):
    def kernel(*refs):
        in_refs, out_refs, sems = refs[: len(arrays)], refs[len(arrays) : -1], refs[-1]
        moves = [
            pltpu.make_async_copy(in_refs[a].at[i], out_refs[r].at[k], sems.at[q])
            for q, (a, i, r, k) in enumerate(copies)
        ]
        for move in moves:
            move.start()
        for move in moves:
            move.wait()

    size = 2 * sum(int(np.prod(shape)) for shape in shapes)
    return pl.pallas_call(
        kernel,
        out_shape=[jax.ShapeDtypeStruct(shape, arrays[0].dtype) for shape in shapes],
        in_specs=[HBM] * len(arrays),
        out_specs=[HBM] * len(shapes),
        scratch_shapes=[pltpu.SemaphoreType.DMA((len(copies),))],
        compiler_params=pltpu.CompilerParams(vmem_limit_bytes=VMEM),
        cost_estimate=pl.CostEstimate(flops=0, bytes_accessed=2 * size, transcendentals=0),
        name=name,
    )(*arrays)


def power_of(top):
    return jnp.floor(jnp.log2(jnp.maximum(top, 1e-30))) + 1.0


def code_tile(tile, power):
    return jnp.round(tile * (jnp.exp2(-power) * CODES)).astype(jnp.int32).astype(jnp.int16)


def top_of(tile):
    return jnp.max(jnp.abs(tile), axis=0, keepdims=True)


def gram_tiles(arrays, pieces, pairs, count):
    rows = arrays[0].shape[-2]
    deep = 8 * rows
    total = len(pieces) * deep
    slots = pairs.shape[0] // 2
    quarter = slots // 4
    strip = 256

    def kernel(pairs_ref, count_ref, *refs):
        array_refs, (out_ref, held, gram, made, powers, sems, out_sems) = refs[:-7], refs[-7:]

        def load(p):
            a, i = pieces[p]
            return pltpu.make_async_copy(array_refs[a].at[i], held.at[pl.ds(p * 8, 8)], sems.at[p])

        def store(t):
            return pltpu.make_async_copy(made.at[t], out_ref.at[t], out_sems.at[t])

        for p in range(len(pieces)):
            load(p).start()
        for p in range(len(pieces)):
            load(p).wait()
            units = pl.ds(p * 8, 8)

            def multiply(m, carry, p=p, units=units):
                lanes = pl.ds(pl.multiple_of(m * strip, strip), strip)
                part = lax.dot_general(
                    held[units, :, lanes].reshape(deep, strip), held[units].reshape(deep, WIDTH),
                    (((0,), (0,)), ((), ())), preferred_element_type=jnp.float32,
                )
                if p == 0:
                    gram[lanes, :] = part
                else:
                    gram[lanes, :] += part
                return carry

            lax.fori_loop(0, WIDTH // strip, multiply, 0)

        for t in range(4):

            def tile_of(k, t=t):
                slot = t * quarter + k
                row = pl.multiple_of(pairs_ref[2 * slot] * BLOCK, BLOCK)
                col = pl.multiple_of(pairs_ref[2 * slot + 1] * BLOCK, BLOCK)
                return jnp.where(slot < count_ref[0], gram[pl.ds(row, BLOCK), pl.ds(col, BLOCK)], 0.0)

            def measure(k, carry, tile_of=tile_of):
                powers[pl.ds(k, 1), :] = top_of(tile_of(k))
                return carry

            def code(k, carry, t=t, tile_of=tile_of):
                span = pl.ds(pl.multiple_of(k * BLOCK, BLOCK), BLOCK)
                made[t, span, :] = code_tile(tile_of(k), powers[pl.ds(k, 1), :])
                return carry

            lax.fori_loop(0, quarter, measure, 0, unroll=4)
            powers[...] = power_of(powers[...])
            lax.fori_loop(0, quarter, code, 0, unroll=2)
            made[t, quarter * BLOCK :, :] = powers[...].astype(jnp.int32).astype(jnp.int16)
            store(t).start()
        for t in range(4):
            store(t).wait()

    return pl.pallas_call(
        kernel,
        out_shape=jax.ShapeDtypeStruct((4, quarter * BLOCK + quarter, BLOCK), jnp.int16),
        grid_spec=pltpu.PrefetchScalarGridSpec(
            num_scalar_prefetch=2,
            grid=(),
            in_specs=[HBM] * len(arrays),
            out_specs=HBM,
            scratch_shapes=[
                pltpu.VMEM((len(pieces) * 8, rows, WIDTH), jnp.bfloat16),
                pltpu.VMEM((WIDTH, WIDTH), jnp.float32),
                pltpu.VMEM((4, quarter * BLOCK + quarter, BLOCK), jnp.int16),
                pltpu.VMEM((quarter, BLOCK), jnp.float32),
                pltpu.SemaphoreType.DMA((len(pieces),)),
                pltpu.SemaphoreType.DMA((4,)),
            ],
        ),
        compiler_params=pltpu.CompilerParams(vmem_limit_bytes=VMEM),
        cost_estimate=pl.CostEstimate(
            flops=2 * total * WIDTH * WIDTH, bytes_accessed=2 * total * WIDTH + 2 * slots * BLOCK * BLOCK,
            transcendentals=0,
        ),
        name="gram_tiles",
    )(pairs, count, *arrays)


def sum_tiles(parts, coded):
    rows = parts[0].shape[1]
    tiles = rows // (BLOCK + 1)
    sources = [(a, q) for a, part in enumerate(parts) for q in range(part.shape[0])]
    last = len(sources) * tiles

    def kernel(*refs):
        part_refs, out_ref, powers, sums = refs[: len(parts)], refs[len(parts)], refs[-2], refs[-1]
        for at, (a, q) in enumerate(sources):
            power = part_refs[a][q, tiles * BLOCK :, :].astype(jnp.int32).astype(jnp.float32)
            powers[at * tiles : (at + 1) * tiles, :] = jnp.exp2(power) * (1.0 / CODES)

        def span_of(k):
            return pl.ds(pl.multiple_of(k * BLOCK, BLOCK), BLOCK)

        def one(k, carry):
            total = None
            for at, (a, q) in enumerate(sources):
                values = part_refs[a][q, span_of(k), :].astype(jnp.int32).astype(jnp.float32)
                term = values * powers[pl.ds(at * tiles + k, 1), :]
                total = term if total is None else total + term
            if coded:
                sums[span_of(k), :] = total
                powers[pl.ds(last + k, 1), :] = top_of(total)
            else:
                out_ref[k] = total
            return carry

        lax.fori_loop(0, tiles, one, 0, unroll=2)
        if coded:
            own = power_of(powers[last:, :])
            powers[last:, :] = own

            def code(k, carry):
                out_ref[0, span_of(k), :] = code_tile(sums[span_of(k), :], powers[pl.ds(last + k, 1), :])
                return carry

            lax.fori_loop(0, tiles, code, 0, unroll=2)
            out_ref[0, tiles * BLOCK :, :] = own.astype(jnp.int32).astype(jnp.int16)

    if coded:
        out = jax.ShapeDtypeStruct((1, rows, BLOCK), jnp.int16)
    else:
        out = jax.ShapeDtypeStruct((tiles, BLOCK, BLOCK), jnp.float32)
    vmem = pl.BlockSpec(memory_space=pltpu.VMEM)
    return pl.pallas_call(
        kernel,
        out_shape=out,
        in_specs=[vmem] * len(parts),
        out_specs=vmem,
        scratch_shapes=[
            pltpu.VMEM((last + tiles, BLOCK), jnp.float32),
            pltpu.VMEM((tiles * BLOCK if coded else 8, BLOCK), jnp.float32),
        ],
        compiler_params=pltpu.CompilerParams(vmem_limit_bytes=VMEM),
        cost_estimate=pl.CostEstimate(
            flops=4 * len(sources) * rows * BLOCK, bytes_accessed=2 * (len(sources) + 2) * rows * BLOCK,
            transcendentals=0,
        ),
        name="sum_tiles",
    )(*parts)


def body(jacobian, obs_weight, block_order, tile_pairs, tile_count):
    rows = jacobian.shape[0]
    planes, lines, cores = lax.axis_size("z"), lax.axis_size("x"), lax.axis_size("c")
    z = lax.axis_index("z")
    weight = jnp.broadcast_to(obs_weight[:, None], (rows, BLOCK))
    group = lines * cores

    dests = [(k % lines, k // lines) for k in range(group)]
    units = [(a, c, (s - FAR) * (1 - 2 * c)) for a, c in dests for s in FAR_STEPS]
    for s in (1, -1):
        units += [(a, c, s) for a, c in dests]
    for s in (2, -2):
        units += [(a, c, s) for a, c in dests if (1 - 2 * c) * s > 0]
    units += [(a, c, 0) for a, c in dests]
    shapes = [(group, len(FAR_STEPS)), (group,), (group,), (lines,), (lines,), (group,)]
    table = np.array(units, np.int32)
    owners = table[:, 0] * (planes * cores) + table[:, 1] + (z + table[:, 2] + planes) % planes * cores

    def up(value, step):
        return lax.ppermute(value, "z", [(b, (b + step) % planes) for b in range(planes)])

    def away(value, step):
        moves = [(b * cores + c, (b + step * (1 - 2 * c)) % planes * cores + c) for b in range(planes) for c in range(cores)]
        return lax.ppermute(value, ("z", "c"), moves)

    def spread(value, axes):
        return lax.all_to_all(value, axes, split_axis=0, concat_axis=0, tiled=True)

    wanted = jnp.concatenate([tile_pairs.reshape(-1), tile_count])
    far_wanted = away(wanted, FAR)

    far, up1, down1, up2, down2, stay = scale_columns(owners.astype(jnp.int32), block_order, jacobian, weight, shapes)
    near_parts = [up(up1, 1), up(down1, -1), up(up2, 2), up(down2, -2), stay]
    far = spread(far, ("c", "x"))
    whole = pl.ds(0, group)
    half = [pl.ds(0, lines), pl.ds(lines, lines)]
    unit = (rows, WIDTH)
    (near,) = copy_parts(
        near_parts,
        [(group, 4, *unit)],
        [(0, whole, 0, (whole, 0)), (1, whole, 0, (whole, 1)), (2, half[0], 0, (half[0], 2)),
         (3, half[0], 0, (half[1], 2)), (4, whole, 0, (whole, 3))],
        "join_near",
    )
    near = spread(near, ("c", "x")).reshape(group * 4, *unit)
    sent = [k for k, s in enumerate(FAR_STEPS) if s]
    far_parts = copy_parts(
        [far], [(group, *unit)] * len(sent), [(0, (whole, k), q, whole) for q, k in enumerate(sent)], "part_far"
    )
    far_parts = [away(part, FAR_STEPS[k]) for part, k in zip(far_parts, sent)]
    far_pieces = [(q, whole) for q in range(len(sent))] + [(len(sent), (whole, FAR_STEPS.index(0)))]
    near_pieces = [(0, pl.ds(8 * q, 8)) for q in range(4)]

    far_tiles = gram_tiles([*far_parts, far], far_pieces, far_wanted[:-1], far_wanted[-1:])
    far_sum = sum_tiles([spread(far_tiles, "y")], True)
    near_tiles = gram_tiles([near], near_pieces, wanted[:-1], wanted[-1:])
    return sum_tiles([spread(near_tiles, "y"), away(far_sum, -FAR)], False)


def solution(mesh):
    shape = (4, mesh.shape["obs"] // 8, 2, mesh.shape["tile"])
    chips = jax.sharding.Mesh(mesh.devices.reshape(shape), ("x", "z", "c", "y"))
    everywhere = ("x", "z", "c", "y")
    owner = ("x", "z", "c")
    return jax.shard_map(
        body,
        mesh=chips,
        in_specs=(P(everywhere, None), P(everywhere), P(), P(owner, None, None), P(owner)),
        out_specs=P(everywhere, None, None),
        check_vma=False,
    )
```

```python
import jax
import jax.numpy as jnp
import numpy as np
from jax import lax
from jax.experimental import pallas as pl
from jax.experimental.pallas import tpu as pltpu
from jax.sharding import PartitionSpec as P

BLOCK = 128
OWN_BLOCKS = 8
WIDTH = OWN_BLOCKS * BLOCK
FAR = 3
FAR_STEPS = (-2, -1, 1, 0)
CODES = 32000.0
VMEM = 62 << 20
HBM = pl.BlockSpec(memory_space=pltpu.HBM)


def scale_columns(owners, order, jacobian, weight, shapes):
    sizes = [int(np.prod(shape)) for shape in shapes]
    units = sum(sizes)
    firsts = np.cumsum([0, *sizes])
    rows, zones = jacobian.shape
    cuts, batch = 8, 4

    def kernel(owners_ref, order_ref, jac_ref, weight_ref, *refs):
        out_refs, (held, made, in_sems, out_sems) = refs[:-4], refs[-4:]
        cut = rows // cuts

        def load(q):
            span = pl.ds(q * cut, cut)
            return pltpu.make_async_copy(jac_ref.at[span], held.at[span], in_sems.at[q])

        def store(q):
            unit = made.at[pl.ds(int(firsts[q]), sizes[q])]
            return pltpu.make_async_copy(unit, out_refs[q], out_sems.at[q])

        for q in range(cuts):
            load(q).start()
        for q in range(cuts):
            load(q).wait()
        root = jnp.sqrt(weight_ref[...])

        def unit(u, carry):
            base = owners_ref[u] * OWN_BLOCKS
            for b in range(OWN_BLOCKS):
                start = pl.multiple_of(order_ref[base + b] * BLOCK, BLOCK)
                piece = held[:, pl.ds(start, BLOCK)].astype(jnp.float32) * root
                made[u, :, b * BLOCK : (b + 1) * BLOCK] = piece.astype(jnp.bfloat16)
            return carry

        for q in range(len(sizes)):
            lax.fori_loop(int(firsts[q]), int(firsts[q + 1]), unit, 0)
            store(q).start()
        for q in range(len(sizes)):
            store(q).wait()

    flat = pl.pallas_call(
        kernel,
        out_shape=[jax.ShapeDtypeStruct((size, rows, WIDTH), jnp.bfloat16) for size in sizes],
        grid_spec=pltpu.PrefetchScalarGridSpec(
            num_scalar_prefetch=2,
            grid=(),
            in_specs=[HBM, pl.BlockSpec(memory_space=pltpu.VMEM)],
            out_specs=[HBM] * len(sizes),
            scratch_shapes=[
                pltpu.VMEM((rows, zones), jnp.bfloat16),
                pltpu.VMEM((units, rows, WIDTH), jnp.bfloat16),
                pltpu.SemaphoreType.DMA((cuts,)),
                pltpu.SemaphoreType.DMA((len(sizes),)),
            ],
        ),
        compiler_params=pltpu.CompilerParams(vmem_limit_bytes=VMEM),
        cost_estimate=pl.CostEstimate(
            flops=units * rows * WIDTH, bytes_accessed=2 * (rows * zones + units * rows * WIDTH), transcendentals=0
        ),
        name="scale_columns",
    )(owners, order, jacobian, weight)
    return [part.reshape(*shape, rows, WIDTH) for part, shape in zip(flat, shapes)]


def copy_parts(arrays, shapes, copies, name):
    def kernel(*refs):
        in_refs, out_refs = refs[: len(arrays)], refs[len(arrays) : len(arrays) + len(shapes)]
        held, (in_sems, out_sems) = refs[len(arrays) + len(shapes) : -2], refs[-2:]

        def load(q):
            a, i, _, _, _ = copies[q]
            return pltpu.make_async_copy(in_refs[a].at[i], held[q], in_sems.at[q])

        def store(q):
            _, _, _, r, k = copies[q]
            return pltpu.make_async_copy(held[q], out_refs[r].at[k], out_sems.at[q])

        for q in range(len(copies)):
            load(q).start()
        for q in range(len(copies)):
            load(q).wait()
            store(q).start()
        for q in range(len(copies)):
            store(q).wait()

    size = 2 * sum(int(np.prod(shape)) for shape in shapes)
    return pl.pallas_call(
        kernel,
        out_shape=[jax.ShapeDtypeStruct(shape, arrays[0].dtype) for shape in shapes],
        in_specs=[HBM] * len(arrays),
        out_specs=[HBM] * len(shapes),
        scratch_shapes=[pltpu.VMEM(shape, arrays[0].dtype) for _, _, shape, _, _ in copies]
        + [pltpu.SemaphoreType.DMA((len(copies),))] * 2,
        compiler_params=pltpu.CompilerParams(vmem_limit_bytes=VMEM),
        cost_estimate=pl.CostEstimate(flops=0, bytes_accessed=2 * size, transcendentals=0),
        name=name,
    )(*arrays)


def power_of(top):
    return jnp.floor(jnp.log2(jnp.maximum(top, 1e-30))) + 1.0


def code_tile(tile, power):
    return jnp.round(tile * (jnp.exp2(-power) * CODES)).astype(jnp.int32).astype(jnp.int16)


def top_of(tile):
    return jnp.max(jnp.abs(tile), axis=0, keepdims=True)


def gram_tiles(arrays, pieces, pairs, count):
    rows = arrays[0].shape[-2]
    deep = 8 * rows
    total = len(pieces) * deep
    slots = pairs.shape[0] // 2
    quarter = slots // 4
    strip = 256

    def kernel(pairs_ref, count_ref, *refs):
        array_refs, (out_ref, held, gram, made, powers, sems, out_sems) = refs[:-7], refs[-7:]

        def load(p):
            a, i = pieces[p]
            return pltpu.make_async_copy(array_refs[a].at[i], held.at[pl.ds(p * 8, 8)], sems.at[p])

        def store(t):
            return pltpu.make_async_copy(made.at[t], out_ref.at[t], out_sems.at[t])

        for p in range(len(pieces)):
            load(p).start()
        for p in range(len(pieces)):
            load(p).wait()
            units = pl.ds(p * 8, 8)

            def multiply(m, carry, p=p, units=units):
                lanes = pl.ds(pl.multiple_of(m * strip, strip), strip)
                part = lax.dot_general(
                    held[units, :, lanes].reshape(deep, strip), held[units].reshape(deep, WIDTH),
                    (((0,), (0,)), ((), ())), preferred_element_type=jnp.float32,
                )
                if p == 0:
                    gram[lanes, :] = part
                else:
                    gram[lanes, :] += part
                return carry

            lax.fori_loop(0, WIDTH // strip, multiply, 0)

        for t in range(4):

            def tile_of(k, t=t):
                slot = t * quarter + k
                row = pl.multiple_of(pairs_ref[2 * slot] * BLOCK, BLOCK)
                col = pl.multiple_of(pairs_ref[2 * slot + 1] * BLOCK, BLOCK)
                return jnp.where(slot < count_ref[0], gram[pl.ds(row, BLOCK), pl.ds(col, BLOCK)], 0.0)

            def measure(k, carry, tile_of=tile_of):
                powers[pl.ds(k, 1), :] = top_of(tile_of(k))
                return carry

            def code(k, carry, t=t, tile_of=tile_of):
                span = pl.ds(pl.multiple_of(k * BLOCK, BLOCK), BLOCK)
                made[t, span, :] = code_tile(tile_of(k), powers[pl.ds(k, 1), :])
                return carry

            lax.fori_loop(0, quarter, measure, 0, unroll=4)
            powers[...] = power_of(powers[...])
            lax.fori_loop(0, quarter, code, 0, unroll=2)
            made[t, quarter * BLOCK :, :] = powers[...].astype(jnp.int32).astype(jnp.int16)
            store(t).start()
        for t in range(4):
            store(t).wait()

    return pl.pallas_call(
        kernel,
        out_shape=jax.ShapeDtypeStruct((4, quarter * BLOCK + quarter, BLOCK), jnp.int16),
        grid_spec=pltpu.PrefetchScalarGridSpec(
            num_scalar_prefetch=2,
            grid=(),
            in_specs=[HBM] * len(arrays),
            out_specs=HBM,
            scratch_shapes=[
                pltpu.VMEM((len(pieces) * 8, rows, WIDTH), jnp.bfloat16),
                pltpu.VMEM((WIDTH, WIDTH), jnp.float32),
                pltpu.VMEM((4, quarter * BLOCK + quarter, BLOCK), jnp.int16),
                pltpu.VMEM((quarter, BLOCK), jnp.float32),
                pltpu.SemaphoreType.DMA((len(pieces),)),
                pltpu.SemaphoreType.DMA((4,)),
            ],
        ),
        compiler_params=pltpu.CompilerParams(vmem_limit_bytes=VMEM),
        cost_estimate=pl.CostEstimate(
            flops=2 * total * WIDTH * WIDTH, bytes_accessed=2 * total * WIDTH + 2 * slots * BLOCK * BLOCK,
            transcendentals=0,
        ),
        name="gram_tiles",
    )(pairs, count, *arrays)


def sum_tiles(parts, coded):
    rows = parts[0].shape[1]
    tiles = rows // (BLOCK + 1)
    sources = [(a, q) for a, part in enumerate(parts) for q in range(part.shape[0])]
    last = len(sources) * tiles

    def kernel(*refs):
        part_refs, out_ref, powers, sums = refs[: len(parts)], refs[len(parts)], refs[-2], refs[-1]
        for at, (a, q) in enumerate(sources):
            power = part_refs[a][q, tiles * BLOCK :, :].astype(jnp.int32).astype(jnp.float32)
            powers[at * tiles : (at + 1) * tiles, :] = jnp.exp2(power) * (1.0 / CODES)

        def span_of(k):
            return pl.ds(pl.multiple_of(k * BLOCK, BLOCK), BLOCK)

        def one(k, carry):
            total = None
            for at, (a, q) in enumerate(sources):
                values = part_refs[a][q, span_of(k), :].astype(jnp.int32).astype(jnp.float32)
                term = values * powers[pl.ds(at * tiles + k, 1), :]
                total = term if total is None else total + term
            if coded:
                sums[span_of(k), :] = total
                powers[pl.ds(last + k, 1), :] = top_of(total)
            else:
                out_ref[k] = total
            return carry

        lax.fori_loop(0, tiles, one, 0, unroll=2)
        if coded:
            own = power_of(powers[last:, :])
            powers[last:, :] = own

            def code(k, carry):
                out_ref[0, span_of(k), :] = code_tile(sums[span_of(k), :], powers[pl.ds(last + k, 1), :])
                return carry

            lax.fori_loop(0, tiles, code, 0, unroll=2)
            out_ref[0, tiles * BLOCK :, :] = own.astype(jnp.int32).astype(jnp.int16)

    if coded:
        out = jax.ShapeDtypeStruct((1, rows, BLOCK), jnp.int16)
    else:
        out = jax.ShapeDtypeStruct((tiles, BLOCK, BLOCK), jnp.float32)
    vmem = pl.BlockSpec(memory_space=pltpu.VMEM)
    return pl.pallas_call(
        kernel,
        out_shape=out,
        in_specs=[vmem] * len(parts),
        out_specs=vmem,
        scratch_shapes=[
            pltpu.VMEM((last + tiles, BLOCK), jnp.float32),
            pltpu.VMEM((tiles * BLOCK if coded else 8, BLOCK), jnp.float32),
        ],
        compiler_params=pltpu.CompilerParams(vmem_limit_bytes=VMEM),
        cost_estimate=pl.CostEstimate(
            flops=4 * len(sources) * rows * BLOCK, bytes_accessed=2 * (len(sources) + 2) * rows * BLOCK,
            transcendentals=0,
        ),
        name="sum_tiles",
    )(*parts)


def body(jacobian, obs_weight, block_order, tile_pairs, tile_count):
    rows = jacobian.shape[0]
    planes, lines, cores = lax.axis_size("z"), lax.axis_size("x"), lax.axis_size("c")
    z = lax.axis_index("z")
    weight = jnp.broadcast_to(obs_weight[:, None], (rows, BLOCK))
    group = lines * cores

    dests = [(k % lines, k // lines) for k in range(group)]
    units = [(a, c, (s - FAR) * (1 - 2 * c)) for a, c in dests for s in FAR_STEPS]
    for s in (1, -1):
        units += [(a, c, s) for a, c in dests]
    for s in (2, -2):
        units += [(a, c, s) for a, c in dests if (1 - 2 * c) * s > 0]
    units += [(a, c, 0) for a, c in dests]
    shapes = [(group, len(FAR_STEPS)), (group,), (group,), (lines,), (lines,), (group,)]
    table = np.array(units, np.int32)
    owners = table[:, 0] * (planes * cores) + table[:, 1] + (z + table[:, 2] + planes) % planes * cores

    def up(value, step):
        return lax.ppermute(value, "z", [(b, (b + step) % planes) for b in range(planes)])

    def away(value, step):
        moves = [(b * cores + c, (b + step * (1 - 2 * c)) % planes * cores + c) for b in range(planes) for c in range(cores)]
        return lax.ppermute(value, ("z", "c"), moves)

    def spread(value, axes):
        return lax.all_to_all(value, axes, split_axis=0, concat_axis=0, tiled=True)

    wanted = jnp.concatenate([tile_pairs.reshape(-1), tile_count])
    far_wanted = away(wanted, FAR)

    far, up1, down1, up2, down2, stay = scale_columns(owners.astype(jnp.int32), block_order, jacobian, weight, shapes)
    near_parts = [up(up1, 1), up(down1, -1), up(up2, 2), up(down2, -2), stay]
    far = spread(far, ("c", "x"))
    whole = pl.ds(0, group)
    half = [pl.ds(0, lines), pl.ds(lines, lines)]
    unit = (rows, WIDTH)
    parts = [(0, 0, 4, 0), (0, 4, 4, 0), (1, 0, 4, 1), (1, 4, 4, 1), (2, 0, 4, 2), (3, 4, 4, 2), (4, 0, 4, 3), (4, 4, 4, 3)]
    (near,) = copy_parts(
        near_parts,
        [(group, 4, *unit)],
        [
            (a, pl.ds(first if near_parts[a].shape[0] == group else 0, n), (n, *unit), 0, (pl.ds(first, n), slot))
            for a, first, n, slot in parts
        ],
        "join_near",
    )
    near = spread(near, ("c", "x")).reshape(group * 4, *unit)
    sent = [k for k, s in enumerate(FAR_STEPS) if s]
    far_parts = copy_parts(
        [far],
        [(group, *unit)] * len(sent),
        [(0, (h, k), (lines, *unit), q, h) for q, k in enumerate(sent) for h in half],
        "part_far",
    )
    far_parts = [away(part, FAR_STEPS[k]) for part, k in zip(far_parts, sent)]
    far_pieces = [(q, whole) for q in range(len(sent))] + [(len(sent), (whole, FAR_STEPS.index(0)))]
    near_pieces = [(0, pl.ds(8 * q, 8)) for q in range(4)]

    far_tiles = gram_tiles([*far_parts, far], far_pieces, far_wanted[:-1], far_wanted[-1:])
    far_sum = sum_tiles([spread(far_tiles, "y")], True)
    near_tiles = gram_tiles([near], near_pieces, wanted[:-1], wanted[-1:])
    return sum_tiles([spread(near_tiles, "y"), away(far_sum, -FAR)], False)


def solution(mesh):
    shape = (4, mesh.shape["obs"] // 8, 2, mesh.shape["tile"])
    chips = jax.sharding.Mesh(mesh.devices.reshape(shape), ("x", "z", "c", "y"))
    everywhere = ("x", "z", "c", "y")
    owner = ("x", "z", "c")
    return jax.shard_map(
        body,
        mesh=chips,
        in_specs=(P(everywhere, None), P(everywhere), P(), P(owner, None, None), P(owner)),
        out_specs=P(everywhere, None, None),
        check_vma=False,
    )
```

```python
import jax
import jax.numpy as jnp
import numpy as np
from jax import lax
from jax.experimental import pallas as pl
from jax.experimental.pallas import tpu as pltpu
from jax.sharding import PartitionSpec as P

BLOCK = 128
OWN_BLOCKS = 8
WIDTH = OWN_BLOCKS * BLOCK
FAR = 3
FAR_FIRST, FAR_THEN = (-2, -1, 0), (1,)
CODES = 32000.0
VMEM = 62 << 20
HBM = pl.BlockSpec(memory_space=pltpu.HBM)


def scale_columns(units, order, jacobian, weight, shapes):
    sizes = [int(np.prod(shape)) for shape in shapes]
    firsts = np.cumsum([0, *sizes])
    total = int(firsts[-1])
    rows, zones = jacobian.shape
    planes, cores = lax.axis_size("z"), lax.axis_size("c")
    halves, cuts = 2, 4

    def kernel(units_ref, order_ref, jac_ref, weight_ref, *refs):
        out_refs, (held, made, in_sems, out_sems) = refs[:-4], refs[-4:]
        half, cut = rows // halves, rows // halves // cuts
        z = lax.axis_index("z")

        def load(h, q):
            span = pl.ds(h * half + q * cut, cut)
            return pltpu.make_async_copy(jac_ref.at[span], held.at[span], in_sems.at[h, q])

        def store(h, q):
            span = pl.ds(h * half, half)
            unit = made.at[pl.ds(int(firsts[q]), sizes[q]), span]
            return pltpu.make_async_copy(unit, out_refs[q].at[:, span], out_sems.at[h, q])

        for h in range(halves):
            for q in range(cuts):
                load(h, q).start()
        row = lax.broadcasted_iota(jnp.int32, (rows, rows), 0)
        col = lax.broadcasted_iota(jnp.int32, (rows, rows), 1)
        root = jnp.sum(jnp.where(row == col, jnp.sqrt(weight_ref[...]), 0.0), axis=1, keepdims=True)
        for h in range(halves):
            for q in range(cuts):
                load(h, q).wait()
            span = pl.ds(h * half, half)
            scale = jnp.broadcast_to(root[h * half : (h + 1) * half], (half, BLOCK))

            def unit(u, carry, span=span, scale=scale):
                what = units_ref[u]
                plane = (z + what % planes) % planes
                base = (what // planes + plane * cores) * OWN_BLOCKS
                for b in range(OWN_BLOCKS):
                    start = pl.multiple_of(order_ref[base + b] * BLOCK, BLOCK)
                    piece = held[span, pl.ds(start, BLOCK)].astype(jnp.float32) * scale
                    made[u, span, b * BLOCK : (b + 1) * BLOCK] = piece.astype(jnp.bfloat16)
                return carry

            for q in range(len(sizes)):
                lax.fori_loop(int(firsts[q]), int(firsts[q + 1]), unit, 0, unroll=2)
                store(h, q).start()
        for h in range(halves):
            for q in range(len(sizes)):
                store(h, q).wait()

    codes = [(a * planes * cores + c) * planes + s % planes for a, c, s in units]
    flat = pl.pallas_call(
        kernel,
        out_shape=[jax.ShapeDtypeStruct((size, rows, WIDTH), jnp.bfloat16) for size in sizes],
        grid_spec=pltpu.PrefetchScalarGridSpec(
            num_scalar_prefetch=2,
            grid=(),
            in_specs=[HBM, pl.BlockSpec(memory_space=pltpu.VMEM)],
            out_specs=[HBM] * len(sizes),
            scratch_shapes=[
                pltpu.VMEM((rows, zones), jnp.bfloat16),
                pltpu.VMEM((total, rows, WIDTH), jnp.bfloat16),
                pltpu.SemaphoreType.DMA((halves, cuts)),
                pltpu.SemaphoreType.DMA((halves, len(sizes))),
            ],
        ),
        compiler_params=pltpu.CompilerParams(vmem_limit_bytes=VMEM),
        cost_estimate=pl.CostEstimate(
            flops=total * rows * WIDTH, bytes_accessed=2 * (rows * zones + total * rows * WIDTH), transcendentals=0
        ),
        name="scale_columns",
    )(jnp.array(codes, jnp.int32), order, jacobian, weight)
    return [part.reshape(*shape, rows, WIDTH) for part, shape in zip(flat, shapes)]


def copy_parts(arrays, shapes, copies, name):
    def kernel(*refs):
        in_refs, out_refs = refs[: len(arrays)], refs[len(arrays) : len(arrays) + len(shapes)]
        held, (in_sems, out_sems) = refs[len(arrays) + len(shapes) : -2], refs[-2:]

        def load(q):
            a, i, _, _, _ = copies[q]
            return pltpu.make_async_copy(in_refs[a].at[i], held[q], in_sems.at[q])

        def store(q):
            _, _, _, r, k = copies[q]
            return pltpu.make_async_copy(held[q], out_refs[r].at[k], out_sems.at[q])

        for q in range(len(copies)):
            load(q).start()
        for q in range(len(copies)):
            load(q).wait()
            store(q).start()
        for q in range(len(copies)):
            store(q).wait()

    size = 2 * sum(int(np.prod(shape)) for shape in shapes)
    return pl.pallas_call(
        kernel,
        out_shape=[jax.ShapeDtypeStruct(shape, arrays[0].dtype) for shape in shapes],
        in_specs=[HBM] * len(arrays),
        out_specs=[HBM] * len(shapes),
        scratch_shapes=[pltpu.VMEM(shape, arrays[0].dtype) for _, _, shape, _, _ in copies]
        + [pltpu.SemaphoreType.DMA((len(copies),))] * 2,
        compiler_params=pltpu.CompilerParams(vmem_limit_bytes=VMEM),
        cost_estimate=pl.CostEstimate(flops=0, bytes_accessed=2 * size, transcendentals=0),
        name=name,
    )(*arrays)


def power_of(top):
    return jnp.floor(jnp.log2(jnp.maximum(top, 1e-30))) + 1.0


def code_tile(tile, power):
    return jnp.round(tile * (jnp.exp2(-power) * CODES)).astype(jnp.int32).astype(jnp.int16)


def top_of(tile):
    return jnp.max(jnp.abs(tile), axis=0, keepdims=True)


def gram_tiles(arrays, pieces, pairs, count, apart):
    rows = arrays[0].shape[-2]
    deep = 8 * rows
    total = len(pieces) * deep
    slots = pairs.shape[0] // 2
    quarter = slots // 4
    strip = 256
    outs = [1, 1, 1, 1] if apart else [4]

    def kernel(pairs_ref, count_ref, *refs):
        array_refs, out_refs, (held, gram, made, powers, sems, out_sems) = refs[: len(arrays)], refs[len(arrays) : -6], refs[-6:]
        own = lax.axis_index("y") if apart else 0

        def load(p):
            a, i = pieces[p]
            return pltpu.make_async_copy(array_refs[a].at[i], held.at[pl.ds(p * 8, 8)], sems.at[p])

        def store(t):
            return pltpu.make_async_copy(made.at[t], out_refs[t].at[0] if apart else out_refs[0].at[t], out_sems.at[t])

        for p in range(len(pieces)):
            load(p).start()
        for p in range(len(pieces)):
            load(p).wait()
            units = pl.ds(p * 8, 8)

            for m in range(0, WIDTH, strip):
                part = lax.dot_general(
                    held[units, :, m : m + strip].reshape(deep, strip), held[units].reshape(deep, WIDTH),
                    (((0,), (0,)), ((), ())), preferred_element_type=jnp.float32,
                )
                if p == 0:
                    gram[m : m + strip, :] = part
                else:
                    gram[m : m + strip, :] += part

        for t in range(4):

            def tile_of(k, t=t):
                slot = (own + t) % 4 * quarter + k
                row = pl.multiple_of(pairs_ref[2 * slot] * BLOCK, BLOCK)
                col = pl.multiple_of(pairs_ref[2 * slot + 1] * BLOCK, BLOCK)
                return jnp.where(slot < count_ref[0], gram[pl.ds(row, BLOCK), pl.ds(col, BLOCK)], 0.0)

            def measure(k, carry, tile_of=tile_of):
                powers[pl.ds(k, 1), :] = top_of(tile_of(k))
                return carry

            def code(k, carry, t=t, tile_of=tile_of):
                span = pl.ds(pl.multiple_of(k * BLOCK, BLOCK), BLOCK)
                made[t, span, :] = code_tile(tile_of(k), powers[pl.ds(k, 1), :])
                return carry

            lax.fori_loop(0, quarter, measure, 0, unroll=4)
            powers[...] = power_of(powers[...])
            lax.fori_loop(0, quarter, code, 0, unroll=2)
            made[t, quarter * BLOCK :, :] = powers[...].astype(jnp.int32).astype(jnp.int16)
            store(t).start()
        for t in range(4):
            store(t).wait()

    return pl.pallas_call(
        kernel,
        out_shape=[jax.ShapeDtypeStruct((n, quarter * BLOCK + quarter, BLOCK), jnp.int16) for n in outs],
        grid_spec=pltpu.PrefetchScalarGridSpec(
            num_scalar_prefetch=2,
            grid=(),
            in_specs=[HBM] * len(arrays),
            out_specs=[HBM] * len(outs),
            scratch_shapes=[
                pltpu.VMEM((len(pieces) * 8, rows, WIDTH), jnp.bfloat16),
                pltpu.VMEM((WIDTH, WIDTH), jnp.float32),
                pltpu.VMEM((4, quarter * BLOCK + quarter, BLOCK), jnp.int16),
                pltpu.VMEM((quarter, BLOCK), jnp.float32),
                pltpu.SemaphoreType.DMA((len(pieces),)),
                pltpu.SemaphoreType.DMA((4,)),
            ],
        ),
        compiler_params=pltpu.CompilerParams(vmem_limit_bytes=VMEM),
        cost_estimate=pl.CostEstimate(
            flops=2 * total * WIDTH * WIDTH, bytes_accessed=2 * total * WIDTH + 2 * slots * BLOCK * BLOCK,
            transcendentals=0,
        ),
        name="gram_tiles",
    )(pairs, count, *arrays)


def sum_tiles(parts, coded):
    rows = parts[0].shape[1]
    tiles = rows // (BLOCK + 1)
    sources = [(a, q) for a, part in enumerate(parts) for q in range(part.shape[0])]
    last = len(sources) * tiles

    def kernel(*refs):
        part_refs, out_ref, powers, sums = refs[: len(parts)], refs[len(parts)], refs[-2], refs[-1]
        for at, (a, q) in enumerate(sources):
            power = part_refs[a][q, tiles * BLOCK :, :].astype(jnp.int32).astype(jnp.float32)
            powers[at * tiles : (at + 1) * tiles, :] = jnp.exp2(power) * (1.0 / CODES)

        def span_of(k):
            return pl.ds(pl.multiple_of(k * BLOCK, BLOCK), BLOCK)

        def one(k, carry):
            total = None
            for at, (a, q) in enumerate(sources):
                values = part_refs[a][q, span_of(k), :].astype(jnp.int32).astype(jnp.float32)
                term = values * powers[pl.ds(at * tiles + k, 1), :]
                total = term if total is None else total + term
            if coded:
                sums[span_of(k), :] = total
                powers[pl.ds(last + k, 1), :] = top_of(total)
            else:
                out_ref[k] = total
            return carry

        lax.fori_loop(0, tiles, one, 0, unroll=2)
        if coded:
            own = power_of(powers[last:, :])
            powers[last:, :] = own

            def code(k, carry):
                out_ref[0, span_of(k), :] = code_tile(sums[span_of(k), :], powers[pl.ds(last + k, 1), :])
                return carry

            lax.fori_loop(0, tiles, code, 0, unroll=2)
            out_ref[0, tiles * BLOCK :, :] = own.astype(jnp.int32).astype(jnp.int16)

    if coded:
        out = jax.ShapeDtypeStruct((1, rows, BLOCK), jnp.int16)
    else:
        out = jax.ShapeDtypeStruct((tiles, BLOCK, BLOCK), jnp.float32)
    vmem = pl.BlockSpec(memory_space=pltpu.VMEM)
    return pl.pallas_call(
        kernel,
        out_shape=out,
        in_specs=[vmem] * len(parts),
        out_specs=vmem,
        scratch_shapes=[
            pltpu.VMEM((last + tiles, BLOCK), jnp.float32),
            pltpu.VMEM((tiles * BLOCK if coded else 8, BLOCK), jnp.float32),
        ],
        compiler_params=pltpu.CompilerParams(vmem_limit_bytes=VMEM),
        cost_estimate=pl.CostEstimate(
            flops=4 * len(sources) * rows * BLOCK, bytes_accessed=2 * (len(sources) + 2) * rows * BLOCK,
            transcendentals=0,
        ),
        name="sum_tiles",
    )(*parts)


def body(jacobian, obs_weight, block_order, tile_pairs, tile_count):
    rows = jacobian.shape[0]
    planes, lines, cores, quarters = (lax.axis_size(name) for name in ("z", "x", "c", "y"))
    group = lines * cores
    weight = obs_weight.reshape(1, rows)

    dests = [(k % lines, k // lines) for k in range(group)]

    def far_units(steps):
        return [(a, c, (s - FAR) * (1 - 2 * c)) for a, c in dests for s in steps]

    def near_units(step, there):
        return [(a, c, step) for a, c in dests if c in there]

    def up(value, step):
        return lax.ppermute(value, "z", [(b, (b + step) % planes) for b in range(planes)])

    def away(value, step):
        moves = [(b * cores + c, (b + step * (1 - 2 * c)) % planes * cores + c) for b in range(planes) for c in range(cores)]
        return lax.ppermute(value, ("z", "c"), moves)

    def spread(value, axes):
        return lax.all_to_all(value, axes, split_axis=0, concat_axis=0, tiled=True)

    def after(value, *others):
        return lax.optimization_barrier((value, *others))[0]

    wanted = jnp.concatenate([tile_pairs.reshape(-1), tile_count])
    far_wanted = away(wanted, FAR)

    units = far_units(FAR_FIRST) + near_units(1, (0, 1)) + near_units(-1, (0, 1)) + near_units(2, (0,)) + near_units(-2, (1,))
    shapes = [(group, len(FAR_FIRST)), (group,), (group,), (lines,), (lines,)]
    far_first, *near_parts = scale_columns(units, block_order, jacobian, weight, shapes)
    weight = after(weight, far_first)
    near_parts = [up(part, step) for part, step in zip(near_parts, (1, -1, 2, -2))]
    units = far_units(FAR_THEN) + near_units(0, (0, 1))
    far_then, stay = scale_columns(units, block_order, jacobian, weight, [(group, len(FAR_THEN)), (group,)])

    unit = (rows, WIDTH)
    whole, half = pl.ds(0, group), [pl.ds(0, lines), pl.ds(lines, lines)]

    def parted(far, steps):
        sent = [k for k, s in enumerate(steps) if s]
        copies = [(0, (h, k), (lines, *unit), q, h) for q, k in enumerate(sent) for h in half]
        parts = copy_parts([far], [(group, *unit)] * len(sent), copies, "part_far")
        return [away(part, steps[k]) for part, k in zip(parts, sent)]

    far_first = spread(far_first, ("c", "x"))
    far_parts = parted(far_first, FAR_FIRST)
    far_then = after(far_then, far_first, *near_parts, far_wanted)
    far_then = spread(far_then, ("c", "x"))
    far_parts += parted(far_then, FAR_THEN)

    pieces = [(0, 0, 4, 0), (0, 4, 4, 0), (1, 0, 4, 1), (1, 4, 4, 1), (2, 0, 4, 2), (3, 4, 4, 2), (4, 0, 4, 3), (4, 4, 4, 3)]
    near_parts.append(stay)
    (near,) = copy_parts(
        near_parts,
        [(group, 4, *unit)],
        [
            (a, pl.ds(first if near_parts[a].shape[0] == group else 0, n), (n, *unit), 0, (pl.ds(first, n), slot))
            for a, first, n, slot in pieces
        ],
        "join_near",
    )
    near = after(near, far_then, far_parts[0])
    near = spread(near, ("c", "x")).reshape(group * 4, *unit)

    far_pieces = [(q, whole) for q in range(len(far_parts))] + [(len(far_parts), (whole, FAR_FIRST.index(0)))]
    far_tiles = list(gram_tiles([*far_parts, far_first], far_pieces, far_wanted[:-1], far_wanted[-1:], True))
    near = after(near, far_tiles[1])
    for k in range(1, quarters):
        far_tiles[k] = lax.ppermute(far_tiles[k], "y", [(b, (b + k) % quarters) for b in range(quarters)])
    near = after(near, far_tiles[1])
    far_sum = away(sum_tiles(far_tiles, True), -FAR)
    near_pieces = [(0, pl.ds(8 * q, 8)) for q in range(4)]
    (near_tiles,) = gram_tiles([near], near_pieces, wanted[:-1], wanted[-1:], False)
    near_tiles = after(near_tiles, *far_tiles[1:])
    return sum_tiles([spread(near_tiles, "y"), far_sum], False)


def solution(mesh):
    shape = (4, mesh.shape["obs"] // 8, 2, mesh.shape["tile"])
    chips = jax.sharding.Mesh(mesh.devices.reshape(shape), ("x", "z", "c", "y"))
    everywhere = ("x", "z", "c", "y")
    owner = ("x", "z", "c")
    return jax.shard_map(
        body,
        mesh=chips,
        in_specs=(P(everywhere, None), P(everywhere), P(), P(owner, None, None), P(owner)),
        out_specs=P(everywhere, None, None),
        check_vma=False,
    )
```

```python
import jax
import jax.numpy as jnp
import numpy as np
from jax import lax
from jax.experimental import pallas as pl
from jax.experimental.pallas import tpu as pltpu
from jax.sharding import PartitionSpec as P

BLOCK = 128
OWN_BLOCKS = 8
WIDTH = OWN_BLOCKS * BLOCK
FAR = 3
FAR_FIRST, FAR_THEN = (-2, -1, 0), (1,)
CODES = 32000.0
VMEM = 62 << 20
HBM = pl.BlockSpec(memory_space=pltpu.HBM)


def scale_columns(units, order, jacobian, weight, shapes):
    sizes = [int(np.prod(shape)) for shape in shapes]
    firsts = np.cumsum([0, *sizes])
    total = int(firsts[-1])
    rows, zones = jacobian.shape
    planes, cores = lax.axis_size("z"), lax.axis_size("c")
    halves, cuts = 2, 4

    def kernel(units_ref, order_ref, jac_ref, weight_ref, *refs):
        out_refs, (held, made, in_sems, out_sems) = refs[:-4], refs[-4:]
        half, cut = rows // halves, rows // halves // cuts
        z = lax.axis_index("z")

        def load(h, q):
            span = pl.ds(h * half + q * cut, cut)
            return pltpu.make_async_copy(jac_ref.at[span], held.at[span], in_sems.at[h, q])

        def store(h, q):
            span = pl.ds(h * half, half)
            unit = made.at[pl.ds(int(firsts[q]), sizes[q]), span]
            return pltpu.make_async_copy(unit, out_refs[q].at[:, span], out_sems.at[h, q])

        for h in range(halves):
            for q in range(cuts):
                load(h, q).start()
        row = lax.broadcasted_iota(jnp.int32, (rows, rows), 0)
        col = lax.broadcasted_iota(jnp.int32, (rows, rows), 1)
        root = jnp.sum(jnp.where(row == col, jnp.sqrt(weight_ref[...]), 0.0), axis=1, keepdims=True)
        for h in range(halves):
            for q in range(cuts):
                load(h, q).wait()
            span = pl.ds(h * half, half)
            scale = jnp.broadcast_to(root[h * half : (h + 1) * half], (half, BLOCK))

            def unit(u, carry, span=span, scale=scale):
                what = units_ref[u]
                plane = (z + what % planes) % planes
                base = (what // planes + plane * cores) * OWN_BLOCKS
                for b in range(OWN_BLOCKS):
                    start = pl.multiple_of(order_ref[base + b] * BLOCK, BLOCK)
                    piece = held[span, pl.ds(start, BLOCK)].astype(jnp.float32) * scale
                    made[u, span, b * BLOCK : (b + 1) * BLOCK] = piece.astype(jnp.bfloat16)
                return carry

            for q in range(len(sizes)):
                lax.fori_loop(int(firsts[q]), int(firsts[q + 1]), unit, 0, unroll=2)
                store(h, q).start()
        for h in range(halves):
            for q in range(len(sizes)):
                store(h, q).wait()

    codes = [(a * planes * cores + c) * planes + s % planes for a, c, s in units]
    flat = pl.pallas_call(
        kernel,
        out_shape=[jax.ShapeDtypeStruct((size, rows, WIDTH), jnp.bfloat16) for size in sizes],
        grid_spec=pltpu.PrefetchScalarGridSpec(
            num_scalar_prefetch=2,
            grid=(),
            in_specs=[HBM, pl.BlockSpec(memory_space=pltpu.VMEM)],
            out_specs=[HBM] * len(sizes),
            scratch_shapes=[
                pltpu.VMEM((rows, zones), jnp.bfloat16),
                pltpu.VMEM((total, rows, WIDTH), jnp.bfloat16),
                pltpu.SemaphoreType.DMA((halves, cuts)),
                pltpu.SemaphoreType.DMA((halves, len(sizes))),
            ],
        ),
        compiler_params=pltpu.CompilerParams(vmem_limit_bytes=VMEM),
        cost_estimate=pl.CostEstimate(
            flops=total * rows * WIDTH, bytes_accessed=2 * (rows * zones + total * rows * WIDTH), transcendentals=0
        ),
        name="scale_columns",
    )(jnp.array(codes, jnp.int32), order, jacobian, weight)
    return [part.reshape(*shape, rows, WIDTH) for part, shape in zip(flat, shapes)]


def copy_parts(arrays, shapes, copies, name):
    def kernel(*refs):
        in_refs, out_refs = refs[: len(arrays)], refs[len(arrays) : len(arrays) + len(shapes)]
        held, (in_sems, out_sems) = refs[len(arrays) + len(shapes) : -2], refs[-2:]

        def load(q):
            a, i, _, _, _ = copies[q]
            return pltpu.make_async_copy(in_refs[a].at[i], held[q], in_sems.at[q])

        def store(q):
            _, _, _, r, k = copies[q]
            return pltpu.make_async_copy(held[q], out_refs[r].at[k], out_sems.at[q])

        for q in range(len(copies)):
            load(q).start()
        for q in range(len(copies)):
            load(q).wait()
            store(q).start()
        for q in range(len(copies)):
            store(q).wait()

    size = 2 * sum(int(np.prod(shape)) for shape in shapes)
    return pl.pallas_call(
        kernel,
        out_shape=[jax.ShapeDtypeStruct(shape, arrays[0].dtype) for shape in shapes],
        in_specs=[HBM] * len(arrays),
        out_specs=[HBM] * len(shapes),
        scratch_shapes=[pltpu.VMEM(shape, arrays[0].dtype) for _, _, shape, _, _ in copies]
        + [pltpu.SemaphoreType.DMA((len(copies),))] * 2,
        compiler_params=pltpu.CompilerParams(vmem_limit_bytes=VMEM),
        cost_estimate=pl.CostEstimate(flops=0, bytes_accessed=2 * size, transcendentals=0),
        name=name,
    )(*arrays)


def power_of(top):
    return jnp.floor(jnp.log2(jnp.maximum(top, 1e-30))) + 1.0


def code_tile(tile, power):
    return jnp.round(tile * (jnp.exp2(-power) * CODES)).astype(jnp.int32).astype(jnp.int16)


def top_of(tile):
    return jnp.max(jnp.abs(tile), axis=0, keepdims=True)


def gram_tiles(arrays, pieces, pairs, count, apart):
    rows = arrays[0].shape[-2]
    deep = 8 * rows
    total = len(pieces) * deep
    slots = pairs.shape[0] // 2
    quarter = slots // 4
    strip = 256
    outs = [1, 1, 1, 1] if apart else [4]

    def kernel(pairs_ref, count_ref, *refs):
        array_refs, out_refs, (held, gram, made, powers, sems, out_sems) = refs[: len(arrays)], refs[len(arrays) : -6], refs[-6:]
        own = lax.axis_index("y") if apart else 0

        def load(p):
            a, i = pieces[p]
            return pltpu.make_async_copy(array_refs[a].at[i], held.at[pl.ds(p * 8, 8)], sems.at[p])

        def store(t):
            return pltpu.make_async_copy(made.at[t], out_refs[t].at[0] if apart else out_refs[0].at[t], out_sems.at[t])

        for p in range(len(pieces)):
            load(p).start()
        for p in range(len(pieces)):
            load(p).wait()
            units = pl.ds(p * 8, 8)

            for m in range(0, WIDTH, strip):
                part = lax.dot_general(
                    held[units, :, m : m + strip].reshape(deep, strip), held[units].reshape(deep, WIDTH),
                    (((0,), (0,)), ((), ())), preferred_element_type=jnp.float32,
                )
                if p == 0:
                    gram[m : m + strip, :] = part
                else:
                    gram[m : m + strip, :] += part

        for t in range(4):

            def tile_of(k, t=t):
                slot = (own + t) % 4 * quarter + k
                row = pl.multiple_of(pairs_ref[2 * slot] * BLOCK, BLOCK)
                col = pl.multiple_of(pairs_ref[2 * slot + 1] * BLOCK, BLOCK)
                return jnp.where(slot < count_ref[0], gram[pl.ds(row, BLOCK), pl.ds(col, BLOCK)], 0.0)

            def measure(k, carry, tile_of=tile_of):
                powers[pl.ds(k, 1), :] = top_of(tile_of(k))
                return carry

            def code(k, carry, t=t, tile_of=tile_of):
                span = pl.ds(pl.multiple_of(k * BLOCK, BLOCK), BLOCK)
                made[t, span, :] = code_tile(tile_of(k), powers[pl.ds(k, 1), :])
                return carry

            lax.fori_loop(0, quarter, measure, 0, unroll=4)
            powers[...] = power_of(powers[...])
            lax.fori_loop(0, quarter, code, 0, unroll=2)
            made[t, quarter * BLOCK :, :] = powers[...].astype(jnp.int32).astype(jnp.int16)
            store(t).start()
        for t in range(4):
            store(t).wait()

    return pl.pallas_call(
        kernel,
        out_shape=[jax.ShapeDtypeStruct((n, quarter * BLOCK + quarter, BLOCK), jnp.int16) for n in outs],
        grid_spec=pltpu.PrefetchScalarGridSpec(
            num_scalar_prefetch=2,
            grid=(),
            in_specs=[HBM] * len(arrays),
            out_specs=[HBM] * len(outs),
            scratch_shapes=[
                pltpu.VMEM((len(pieces) * 8, rows, WIDTH), jnp.bfloat16),
                pltpu.VMEM((WIDTH, WIDTH), jnp.float32),
                pltpu.VMEM((4, quarter * BLOCK + quarter, BLOCK), jnp.int16),
                pltpu.VMEM((quarter, BLOCK), jnp.float32),
                pltpu.SemaphoreType.DMA((len(pieces),)),
                pltpu.SemaphoreType.DMA((4,)),
            ],
        ),
        compiler_params=pltpu.CompilerParams(vmem_limit_bytes=VMEM),
        cost_estimate=pl.CostEstimate(
            flops=2 * total * WIDTH * WIDTH, bytes_accessed=2 * total * WIDTH + 2 * slots * BLOCK * BLOCK,
            transcendentals=0,
        ),
        name="gram_tiles",
    )(pairs, count, *arrays)


def sum_tiles(parts, coded):
    rows = parts[0].shape[1]
    tiles = rows // (BLOCK + 1)
    sources = [(a, q) for a, part in enumerate(parts) for q in range(part.shape[0])]
    last = len(sources) * tiles

    def kernel(*refs):
        part_refs, out_ref, powers, sums = refs[: len(parts)], refs[len(parts)], refs[-2], refs[-1]
        for at, (a, q) in enumerate(sources):
            power = part_refs[a][q, tiles * BLOCK :, :].astype(jnp.int32).astype(jnp.float32)
            powers[at * tiles : (at + 1) * tiles, :] = jnp.exp2(power) * (1.0 / CODES)

        def span_of(k):
            return pl.ds(pl.multiple_of(k * BLOCK, BLOCK), BLOCK)

        def one(k, carry):
            total = None
            for at, (a, q) in enumerate(sources):
                values = part_refs[a][q, span_of(k), :].astype(jnp.int32).astype(jnp.float32)
                term = values * powers[pl.ds(at * tiles + k, 1), :]
                total = term if total is None else total + term
            if coded:
                sums[span_of(k), :] = total
                powers[pl.ds(last + k, 1), :] = top_of(total)
            else:
                out_ref[k] = total
            return carry

        lax.fori_loop(0, tiles, one, 0, unroll=2)
        if coded:
            own = power_of(powers[last:, :])
            powers[last:, :] = own

            def code(k, carry):
                out_ref[0, span_of(k), :] = code_tile(sums[span_of(k), :], powers[pl.ds(last + k, 1), :])
                return carry

            lax.fori_loop(0, tiles, code, 0, unroll=2)
            out_ref[0, tiles * BLOCK :, :] = own.astype(jnp.int32).astype(jnp.int16)

    if coded:
        out = jax.ShapeDtypeStruct((1, rows, BLOCK), jnp.int16)
    else:
        out = jax.ShapeDtypeStruct((tiles, BLOCK, BLOCK), jnp.float32)
    vmem = pl.BlockSpec(memory_space=pltpu.VMEM)
    return pl.pallas_call(
        kernel,
        out_shape=out,
        in_specs=[vmem] * len(parts),
        out_specs=vmem,
        scratch_shapes=[
            pltpu.VMEM((last + tiles, BLOCK), jnp.float32),
            pltpu.VMEM((tiles * BLOCK if coded else 8, BLOCK), jnp.float32),
        ],
        compiler_params=pltpu.CompilerParams(vmem_limit_bytes=VMEM),
        cost_estimate=pl.CostEstimate(
            flops=4 * len(sources) * rows * BLOCK, bytes_accessed=2 * (len(sources) + 2) * rows * BLOCK,
            transcendentals=0,
        ),
        name="sum_tiles",
    )(*parts)


def body(jacobian, obs_weight, block_order, tile_pairs, tile_count):
    rows = jacobian.shape[0]
    planes, lines, cores, quarters = (lax.axis_size(name) for name in ("z", "x", "c", "y"))
    group = lines * cores
    weight = obs_weight.reshape(1, rows)

    dests = [(k % lines, k // lines) for k in range(group)]

    def far_units(steps):
        return [(a, c, (s - FAR) * (1 - 2 * c)) for a, c in dests for s in steps]

    def near_units(step, there):
        return [(a, c, step) for a, c in dests if c in there]

    def up(value, step):
        return lax.ppermute(value, "z", [(b, (b + step) % planes) for b in range(planes)])

    def away(value, step):
        moves = [(b * cores + c, (b + step * (1 - 2 * c)) % planes * cores + c) for b in range(planes) for c in range(cores)]
        return lax.ppermute(value, ("z", "c"), moves)

    def spread(value, axes):
        return lax.all_to_all(value, axes, split_axis=0, concat_axis=0, tiled=True)

    def after(value, *others):
        return lax.optimization_barrier((value, *others))[0]

    wanted = jnp.concatenate([tile_pairs.reshape(-1), tile_count])
    far_wanted = away(wanted, FAR)

    units = far_units(FAR_FIRST) + near_units(1, (0, 1)) + near_units(-1, (0, 1)) + near_units(2, (0,)) + near_units(-2, (1,))
    shapes = [(group, len(FAR_FIRST)), (group,), (group,), (lines,), (lines,)]
    far_first, *near_parts = scale_columns(units, block_order, jacobian, weight, shapes)
    weight = after(weight, far_first)
    near_parts = [up(part, step) for part, step in zip(near_parts, (1, -1, 2, -2))]
    units = far_units(FAR_THEN) + near_units(0, (0, 1))
    far_then, stay = scale_columns(units, block_order, jacobian, weight, [(group, len(FAR_THEN)), (group,)])

    unit = (rows, WIDTH)
    whole, half = pl.ds(0, group), [pl.ds(0, lines), pl.ds(lines, lines)]

    def parted(far, steps):
        sent = [k for k, s in enumerate(steps) if s]
        copies = [(0, (h, k), (lines, *unit), q, h) for q, k in enumerate(sent) for h in half]
        parts = copy_parts([far], [(group, *unit)] * len(sent), copies, "part_far")
        return [away(part, steps[k]) for part, k in zip(parts, sent)]

    far_first = spread(far_first, ("c", "x"))
    far_first = after(far_first, stay)
    far_parts = parted(far_first, FAR_FIRST)
    far_then = after(far_then, far_first, *near_parts)
    far_then = spread(far_then, ("c", "x"))
    far_parts += parted(far_then, FAR_THEN)

    pieces = [(0, 0, 4, 0), (0, 4, 4, 0), (1, 0, 4, 1), (1, 4, 4, 1), (2, 0, 4, 2), (3, 4, 4, 2), (4, 0, 4, 3), (4, 4, 4, 3)]
    near_parts.append(stay)
    (near,) = copy_parts(
        near_parts,
        [(group, 4, *unit)],
        [
            (a, pl.ds(first if near_parts[a].shape[0] == group else 0, n), (n, *unit), 0, (pl.ds(first, n), slot))
            for a, first, n, slot in pieces
        ],
        "join_near",
    )
    near = after(near, far_then, far_parts[0], far_wanted)
    near = spread(near, ("c", "x")).reshape(group * 4, *unit)

    far_pieces = [(q, whole) for q in range(len(far_parts))] + [(len(far_parts), (whole, FAR_FIRST.index(0)))]
    far_tiles = list(gram_tiles([*far_parts, far_first], far_pieces, far_wanted[:-1], far_wanted[-1:], True))
    near = after(near, far_tiles[1])
    for k in range(1, quarters):
        far_tiles[k] = lax.ppermute(far_tiles[k], "y", [(b, (b + k) % quarters) for b in range(quarters)])
    far_sum = away(sum_tiles(far_tiles, True), -FAR)
    near_pieces = [(0, pl.ds(8 * q, 8)) for q in range(4)]
    (near_tiles,) = gram_tiles([near], near_pieces, wanted[:-1], wanted[-1:], False)
    near_tiles = after(near_tiles, *far_tiles[1:])
    return sum_tiles([spread(near_tiles, "y"), far_sum], False)


def solution(mesh):
    shape = (4, mesh.shape["obs"] // 8, 2, mesh.shape["tile"])
    chips = jax.sharding.Mesh(mesh.devices.reshape(shape), ("x", "z", "c", "y"))
    everywhere = ("x", "z", "c", "y")
    owner = ("x", "z", "c")
    return jax.shard_map(
        body,
        mesh=chips,
        in_specs=(P(everywhere, None), P(everywhere), P(), P(owner, None, None), P(owner)),
        out_specs=P(everywhere, None, None),
        check_vma=False,
    )
```

```python
import jax
import jax.numpy as jnp
import numpy as np
from jax import lax
from jax.experimental import pallas as pl
from jax.experimental.pallas import tpu as pltpu
from jax.sharding import PartitionSpec as P

BLOCK = 128
OWN_BLOCKS = 8
WIDTH = OWN_BLOCKS * BLOCK
FAR = 3
FAR_FIRST, FAR_THEN = (-2, -1, 0), (1,)
CODES = 32000.0
VMEM = 62 << 20
HBM = pl.BlockSpec(memory_space=pltpu.HBM)


def scale_columns(units, order, jacobian, weight, shapes):
    sizes = [int(np.prod(shape)) for shape in shapes]
    firsts = np.cumsum([0, *sizes])
    total = int(firsts[-1])
    rows, zones = jacobian.shape
    planes, cores = lax.axis_size("z"), lax.axis_size("c")
    halves, cuts = 2, 4

    def kernel(units_ref, order_ref, jac_ref, weight_ref, *refs):
        out_refs, (held, made, in_sems, out_sems) = refs[:-4], refs[-4:]
        half, cut = rows // halves, rows // halves // cuts
        z = lax.axis_index("z")

        def load(h, q):
            span = pl.ds(h * half + q * cut, cut)
            return pltpu.make_async_copy(jac_ref.at[span], held.at[span], in_sems.at[h, q])

        def store(h, q):
            span = pl.ds(h * half, half)
            unit = made.at[pl.ds(int(firsts[q]), sizes[q]), span]
            return pltpu.make_async_copy(unit, out_refs[q].at[:, span], out_sems.at[h, q])

        for h in range(halves):
            for q in range(cuts):
                load(h, q).start()
        row = lax.broadcasted_iota(jnp.int32, (rows, rows), 0)
        col = lax.broadcasted_iota(jnp.int32, (rows, rows), 1)
        root = jnp.sum(jnp.where(row == col, jnp.sqrt(weight_ref[...]), 0.0), axis=1, keepdims=True)
        for h in range(halves):
            for q in range(cuts):
                load(h, q).wait()
            span = pl.ds(h * half, half)
            scale = jnp.broadcast_to(root[h * half : (h + 1) * half], (half, BLOCK))

            def unit(u, carry, span=span, scale=scale):
                what = units_ref[u]
                plane = (z + what % planes) % planes
                base = (what // planes + plane * cores) * OWN_BLOCKS
                for b in range(OWN_BLOCKS):
                    start = pl.multiple_of(order_ref[base + b] * BLOCK, BLOCK)
                    piece = held[span, pl.ds(start, BLOCK)].astype(jnp.float32) * scale
                    made[u, span, b * BLOCK : (b + 1) * BLOCK] = piece.astype(jnp.bfloat16)
                return carry

            for q in range(len(sizes)):
                lax.fori_loop(int(firsts[q]), int(firsts[q + 1]), unit, 0, unroll=2)
                store(h, q).start()
        for h in range(halves):
            for q in range(len(sizes)):
                store(h, q).wait()

    codes = [(a * planes * cores + c) * planes + s % planes for a, c, s in units]
    flat = pl.pallas_call(
        kernel,
        out_shape=[jax.ShapeDtypeStruct((size, rows, WIDTH), jnp.bfloat16) for size in sizes],
        grid_spec=pltpu.PrefetchScalarGridSpec(
            num_scalar_prefetch=2,
            grid=(),
            in_specs=[HBM, pl.BlockSpec(memory_space=pltpu.VMEM)],
            out_specs=[HBM] * len(sizes),
            scratch_shapes=[
                pltpu.VMEM((rows, zones), jnp.bfloat16),
                pltpu.VMEM((total, rows, WIDTH), jnp.bfloat16),
                pltpu.SemaphoreType.DMA((halves, cuts)),
                pltpu.SemaphoreType.DMA((halves, len(sizes))),
            ],
        ),
        compiler_params=pltpu.CompilerParams(vmem_limit_bytes=VMEM),
        cost_estimate=pl.CostEstimate(
            flops=total * rows * WIDTH, bytes_accessed=2 * (rows * zones + total * rows * WIDTH), transcendentals=0
        ),
        name="scale_columns",
    )(jnp.array(codes, jnp.int32), order, jacobian, weight)
    return [part.reshape(*shape, rows, WIDTH) for part, shape in zip(flat, shapes)]


def copy_parts(arrays, shapes, copies, name):
    def kernel(*refs):
        in_refs, out_refs = refs[: len(arrays)], refs[len(arrays) : len(arrays) + len(shapes)]
        held, (in_sems, out_sems) = refs[len(arrays) + len(shapes) : -2], refs[-2:]

        def load(q):
            a, i, _, _, _ = copies[q]
            return pltpu.make_async_copy(in_refs[a].at[i], held[q], in_sems.at[q])

        def store(q):
            _, _, _, r, k = copies[q]
            return pltpu.make_async_copy(held[q], out_refs[r].at[k], out_sems.at[q])

        for q in range(len(copies)):
            load(q).start()
        for q in range(len(copies)):
            load(q).wait()
            store(q).start()
        for q in range(len(copies)):
            store(q).wait()

    size = 2 * sum(int(np.prod(shape)) for shape in shapes)
    return pl.pallas_call(
        kernel,
        out_shape=[jax.ShapeDtypeStruct(shape, arrays[0].dtype) for shape in shapes],
        in_specs=[HBM] * len(arrays),
        out_specs=[HBM] * len(shapes),
        scratch_shapes=[pltpu.VMEM(shape, arrays[0].dtype) for _, _, shape, _, _ in copies]
        + [pltpu.SemaphoreType.DMA((len(copies),))] * 2,
        compiler_params=pltpu.CompilerParams(vmem_limit_bytes=VMEM),
        cost_estimate=pl.CostEstimate(flops=0, bytes_accessed=2 * size, transcendentals=0),
        name=name,
    )(*arrays)


def power_of(top):
    return jnp.floor(jnp.log2(jnp.maximum(top, 1e-30))) + 1.0


def code_tile(tile, power):
    return jnp.round(tile * (jnp.exp2(-power) * CODES)).astype(jnp.int32).astype(jnp.int16)


def top_of(tile):
    return jnp.max(jnp.abs(tile), axis=0, keepdims=True)


def gram_tiles(arrays, pieces, pairs, count, apart):
    rows = arrays[0].shape[-2]
    deep = 8 * rows
    total = len(pieces) * deep
    slots = pairs.shape[0] // 2
    quarter = slots // 4
    strip = 256
    outs = [1, 1, 1, 1] if apart else [4]

    def kernel(pairs_ref, count_ref, *refs):
        array_refs, out_refs, (held, gram, made, powers, sems, out_sems) = refs[: len(arrays)], refs[len(arrays) : -6], refs[-6:]
        own = lax.axis_index("y") if apart else 0

        def load(p):
            a, i = pieces[p]
            return pltpu.make_async_copy(array_refs[a].at[i], held.at[pl.ds(p * 8, 8)], sems.at[p])

        def store(t):
            return pltpu.make_async_copy(made.at[t], out_refs[t].at[0] if apart else out_refs[0].at[t], out_sems.at[t])

        for p in range(len(pieces)):
            load(p).start()
        for p in range(len(pieces)):
            load(p).wait()
            units = pl.ds(p * 8, 8)

            for m in range(0, WIDTH, strip):
                part = lax.dot_general(
                    held[units, :, m : m + strip].reshape(deep, strip), held[units].reshape(deep, WIDTH),
                    (((0,), (0,)), ((), ())), preferred_element_type=jnp.float32,
                )
                if p == 0:
                    gram[m : m + strip, :] = part
                else:
                    gram[m : m + strip, :] += part

        for t in range(4):

            def tile_of(k, t=t):
                slot = (own + t) % 4 * quarter + k
                row = pl.multiple_of(pairs_ref[2 * slot] * BLOCK, BLOCK)
                col = pl.multiple_of(pairs_ref[2 * slot + 1] * BLOCK, BLOCK)
                return jnp.where(slot < count_ref[0], gram[pl.ds(row, BLOCK), pl.ds(col, BLOCK)], 0.0)

            def measure(k, carry, tile_of=tile_of):
                powers[pl.ds(k, 1), :] = top_of(tile_of(k))
                return carry

            def code(k, carry, t=t, tile_of=tile_of):
                span = pl.ds(pl.multiple_of(k * BLOCK, BLOCK), BLOCK)
                made[t, span, :] = code_tile(tile_of(k), powers[pl.ds(k, 1), :])
                return carry

            lax.fori_loop(0, quarter, measure, 0, unroll=4)
            powers[...] = power_of(powers[...])
            lax.fori_loop(0, quarter, code, 0, unroll=2)
            made[t, quarter * BLOCK :, :] = powers[...].astype(jnp.int32).astype(jnp.int16)
            store(t).start()
        for t in range(4):
            store(t).wait()

    return pl.pallas_call(
        kernel,
        out_shape=[jax.ShapeDtypeStruct((n, quarter * BLOCK + quarter, BLOCK), jnp.int16) for n in outs],
        grid_spec=pltpu.PrefetchScalarGridSpec(
            num_scalar_prefetch=2,
            grid=(),
            in_specs=[HBM] * len(arrays),
            out_specs=[HBM] * len(outs),
            scratch_shapes=[
                pltpu.VMEM((len(pieces) * 8, rows, WIDTH), jnp.bfloat16),
                pltpu.VMEM((WIDTH, WIDTH), jnp.float32),
                pltpu.VMEM((4, quarter * BLOCK + quarter, BLOCK), jnp.int16),
                pltpu.VMEM((quarter, BLOCK), jnp.float32),
                pltpu.SemaphoreType.DMA((len(pieces),)),
                pltpu.SemaphoreType.DMA((4,)),
            ],
        ),
        compiler_params=pltpu.CompilerParams(vmem_limit_bytes=VMEM),
        cost_estimate=pl.CostEstimate(
            flops=2 * total * WIDTH * WIDTH, bytes_accessed=2 * total * WIDTH + 2 * slots * BLOCK * BLOCK,
            transcendentals=0,
        ),
        name="gram_tiles",
    )(pairs, count, *arrays)


def sum_tiles(parts, coded):
    rows = parts[0].shape[1]
    tiles = rows // (BLOCK + 1)
    sources = [(a, q) for a, part in enumerate(parts) for q in range(part.shape[0])]
    last = len(sources) * tiles

    def kernel(*refs):
        part_refs, out_ref, powers, sums = refs[: len(parts)], refs[len(parts)], refs[-2], refs[-1]
        for at, (a, q) in enumerate(sources):
            power = part_refs[a][q, tiles * BLOCK :, :].astype(jnp.int32).astype(jnp.float32)
            powers[at * tiles : (at + 1) * tiles, :] = jnp.exp2(power) * (1.0 / CODES)

        def span_of(k):
            return pl.ds(pl.multiple_of(k * BLOCK, BLOCK), BLOCK)

        def one(k, carry):
            total = None
            for at, (a, q) in enumerate(sources):
                values = part_refs[a][q, span_of(k), :].astype(jnp.int32).astype(jnp.float32)
                term = values * powers[pl.ds(at * tiles + k, 1), :]
                total = term if total is None else total + term
            if coded:
                sums[span_of(k), :] = total
                powers[pl.ds(last + k, 1), :] = top_of(total)
            else:
                out_ref[k] = total
            return carry

        lax.fori_loop(0, tiles, one, 0, unroll=2)
        if coded:
            own = power_of(powers[last:, :])
            powers[last:, :] = own

            def code(k, carry):
                out_ref[0, span_of(k), :] = code_tile(sums[span_of(k), :], powers[pl.ds(last + k, 1), :])
                return carry

            lax.fori_loop(0, tiles, code, 0, unroll=2)
            out_ref[0, tiles * BLOCK :, :] = own.astype(jnp.int32).astype(jnp.int16)

    if coded:
        out = jax.ShapeDtypeStruct((1, rows, BLOCK), jnp.int16)
    else:
        out = jax.ShapeDtypeStruct((tiles, BLOCK, BLOCK), jnp.float32)
    vmem = pl.BlockSpec(memory_space=pltpu.VMEM)
    return pl.pallas_call(
        kernel,
        out_shape=out,
        in_specs=[vmem] * len(parts),
        out_specs=vmem,
        scratch_shapes=[
            pltpu.VMEM((last + tiles, BLOCK), jnp.float32),
            pltpu.VMEM((tiles * BLOCK if coded else 8, BLOCK), jnp.float32),
        ],
        compiler_params=pltpu.CompilerParams(vmem_limit_bytes=VMEM),
        cost_estimate=pl.CostEstimate(
            flops=4 * len(sources) * rows * BLOCK, bytes_accessed=2 * (len(sources) + 2) * rows * BLOCK,
            transcendentals=0,
        ),
        name="sum_tiles",
    )(*parts)


def body(jacobian, obs_weight, block_order, tile_pairs, tile_count):
    rows = jacobian.shape[0]
    planes, lines, cores, quarters = (lax.axis_size(name) for name in ("z", "x", "c", "y"))
    group = lines * cores
    weight = obs_weight.reshape(1, rows)

    dests = [(k % lines, k // lines) for k in range(group)]

    def far_units(steps):
        return [(a, c, (s - FAR) * (1 - 2 * c)) for a, c in dests for s in steps]

    def near_units(step, there):
        return [(a, c, step) for a, c in dests if c in there]

    def up(value, step):
        return lax.ppermute(value, "z", [(b, (b + step) % planes) for b in range(planes)])

    def away(value, step):
        moves = [(b * cores + c, (b + step * (1 - 2 * c)) % planes * cores + c) for b in range(planes) for c in range(cores)]
        return lax.ppermute(value, ("z", "c"), moves)

    def spread(value, axes):
        return lax.all_to_all(value, axes, split_axis=0, concat_axis=0, tiled=True)

    def after(value, *others):
        return lax.optimization_barrier((value, *others))[0]

    wanted = jnp.concatenate([tile_pairs.reshape(-1), tile_count])
    far_wanted = away(wanted, FAR)

    units = far_units(FAR_FIRST) + near_units(1, (0, 1)) + near_units(-1, (0, 1)) + near_units(2, (0,)) + near_units(-2, (1,))
    shapes = [(group, len(FAR_FIRST)), (group,), (group,), (lines,), (lines,)]
    far_first, *near_parts = scale_columns(units, block_order, jacobian, weight, shapes)
    weight = after(weight, far_first)
    near_parts = [up(part, step) for part, step in zip(near_parts, (1, -1, 2, -2))]
    units = far_units(FAR_THEN) + near_units(0, (0, 1))
    far_then, stay = scale_columns(units, block_order, jacobian, weight, [(group, len(FAR_THEN)), (group,)])

    unit = (rows, WIDTH)
    whole, half = pl.ds(0, group), [pl.ds(0, lines), pl.ds(lines, lines)]

    def parted(far, steps):
        sent = [k for k, s in enumerate(steps) if s]
        copies = [(0, (h, k), (lines, *unit), q, h) for q, k in enumerate(sent) for h in half]
        parts = copy_parts([far], [(group, *unit)] * len(sent), copies, "part_far")
        return [away(part, steps[k] // abs(steps[k])) for part, k in zip(parts, sent)]

    far_first = spread(far_first, ("c", "x"))
    far_first = after(far_first, stay)
    far_parts = parted(far_first, FAR_FIRST)
    far_then = after(far_then, far_first, *near_parts)
    far_then = spread(far_then, ("c", "x"))
    far_parts += parted(far_then, FAR_THEN)

    pieces = [(0, 0, 4, 0), (0, 4, 4, 0), (1, 0, 4, 1), (1, 4, 4, 1), (2, 0, 4, 2), (3, 4, 4, 2), (4, 0, 4, 3), (4, 4, 4, 3)]
    near_parts.append(stay)
    (near,) = copy_parts(
        near_parts,
        [(group, 4, *unit)],
        [
            (a, pl.ds(first if near_parts[a].shape[0] == group else 0, n), (n, *unit), 0, (pl.ds(first, n), slot))
            for a, first, n, slot in pieces
        ],
        "join_near",
    )
    near = after(near, far_then, far_parts[0], far_parts[1], far_wanted)
    far_parts[0] = away(far_parts[0], -1)
    near = spread(near, ("c", "x")).reshape(group * 4, *unit)

    far_pieces = [(q, whole) for q in range(len(far_parts))] + [(len(far_parts), (whole, FAR_FIRST.index(0)))]
    far_tiles = list(gram_tiles([*far_parts, far_first], far_pieces, far_wanted[:-1], far_wanted[-1:], True))
    near = after(near, far_tiles[1])
    for k in range(1, quarters):
        far_tiles[k] = lax.ppermute(far_tiles[k], "y", [(b, (b + k) % quarters) for b in range(quarters)])
    far_sum = away(sum_tiles(far_tiles, True), -FAR)
    near_pieces = [(0, pl.ds(8 * q, 8)) for q in range(4)]
    (near_tiles,) = gram_tiles([near], near_pieces, wanted[:-1], wanted[-1:], False)
    near_tiles = after(near_tiles, *far_tiles[1:])
    return sum_tiles([spread(near_tiles, "y"), far_sum], False)


def solution(mesh):
    shape = (4, mesh.shape["obs"] // 8, 2, mesh.shape["tile"])
    chips = jax.sharding.Mesh(mesh.devices.reshape(shape), ("x", "z", "c", "y"))
    everywhere = ("x", "z", "c", "y")
    owner = ("x", "z", "c")
    return jax.shard_map(
        body,
        mesh=chips,
        in_specs=(P(everywhere, None), P(everywhere), P(), P(owner, None, None), P(owner)),
        out_specs=P(everywhere, None, None),
        check_vma=False,
    )
```

```python
import jax
import jax.numpy as jnp
import numpy as np
from jax import lax
from jax.experimental import pallas as pl
from jax.experimental.pallas import tpu as pltpu
from jax.sharding import PartitionSpec as P

BLOCK = 128
OWN_BLOCKS = 8
WIDTH = OWN_BLOCKS * BLOCK
FAR = 3
FAR_FIRST, FAR_THEN = (-2, -1, 0), (1,)
CODES = 32000.0
VMEM = 62 << 20
HBM = pl.BlockSpec(memory_space=pltpu.HBM)


def scale_columns(units, order, jacobian, weight, shapes):
    sizes = [int(np.prod(shape)) for shape in shapes]
    firsts = np.cumsum([0, *sizes])
    total = int(firsts[-1])
    rows, zones = jacobian.shape
    planes, cores = lax.axis_size("z"), lax.axis_size("c")
    halves, cuts = 2, 4

    def kernel(units_ref, order_ref, jac_ref, weight_ref, *refs):
        out_refs, (held, made, in_sems, out_sems) = refs[:-4], refs[-4:]
        half, cut = rows // halves, rows // halves // cuts
        z = lax.axis_index("z")

        def load(h, q):
            span = pl.ds(h * half + q * cut, cut)
            return pltpu.make_async_copy(jac_ref.at[span], held.at[span], in_sems.at[h, q])

        def store(h, q):
            span = pl.ds(h * half, half)
            unit = made.at[pl.ds(int(firsts[q]), sizes[q]), span]
            return pltpu.make_async_copy(unit, out_refs[q].at[:, span], out_sems.at[h, q])

        for h in range(halves):
            for q in range(cuts):
                load(h, q).start()
        row = lax.broadcasted_iota(jnp.int32, (rows, rows), 0)
        col = lax.broadcasted_iota(jnp.int32, (rows, rows), 1)
        root = jnp.sum(jnp.where(row == col, jnp.sqrt(weight_ref[...]), 0.0), axis=1, keepdims=True)
        for h in range(halves):
            for q in range(cuts):
                load(h, q).wait()
            span = pl.ds(h * half, half)
            scale = jnp.broadcast_to(root[h * half : (h + 1) * half], (half, BLOCK))

            def unit(u, carry, span=span, scale=scale):
                what = units_ref[u]
                plane = (z + what % planes) % planes
                base = (what // planes + plane * cores) * OWN_BLOCKS
                for b in range(OWN_BLOCKS):
                    start = pl.multiple_of(order_ref[base + b] * BLOCK, BLOCK)
                    piece = held[span, pl.ds(start, BLOCK)].astype(jnp.float32) * scale
                    made[u, span, b * BLOCK : (b + 1) * BLOCK] = piece.astype(jnp.bfloat16)
                return carry

            for q in range(len(sizes)):
                lax.fori_loop(int(firsts[q]), int(firsts[q + 1]), unit, 0, unroll=2)
                store(h, q).start()
        for h in range(halves):
            for q in range(len(sizes)):
                store(h, q).wait()

    codes = [(a * planes * cores + c) * planes + s % planes for a, c, s in units]
    flat = pl.pallas_call(
        kernel,
        out_shape=[jax.ShapeDtypeStruct((size, rows, WIDTH), jnp.bfloat16) for size in sizes],
        grid_spec=pltpu.PrefetchScalarGridSpec(
            num_scalar_prefetch=2,
            grid=(),
            in_specs=[HBM, pl.BlockSpec(memory_space=pltpu.VMEM)],
            out_specs=[HBM] * len(sizes),
            scratch_shapes=[
                pltpu.VMEM((rows, zones), jnp.bfloat16),
                pltpu.VMEM((total, rows, WIDTH), jnp.bfloat16),
                pltpu.SemaphoreType.DMA((halves, cuts)),
                pltpu.SemaphoreType.DMA((halves, len(sizes))),
            ],
        ),
        compiler_params=pltpu.CompilerParams(vmem_limit_bytes=VMEM),
        cost_estimate=pl.CostEstimate(
            flops=total * rows * WIDTH, bytes_accessed=2 * (rows * zones + total * rows * WIDTH), transcendentals=0
        ),
        name="scale_columns",
    )(jnp.array(codes, jnp.int32), order, jacobian, weight)
    return [part.reshape(*shape, rows, WIDTH) for part, shape in zip(flat, shapes)]


def copy_parts(arrays, shapes, copies, name):
    def kernel(*refs):
        in_refs, out_refs = refs[: len(arrays)], refs[len(arrays) : len(arrays) + len(shapes)]
        held, (in_sems, out_sems) = refs[len(arrays) + len(shapes) : -2], refs[-2:]

        def load(q):
            a, i, _, _, _ = copies[q]
            return pltpu.make_async_copy(in_refs[a].at[i], held[q], in_sems.at[q])

        def store(q):
            _, _, _, r, k = copies[q]
            return pltpu.make_async_copy(held[q], out_refs[r].at[k], out_sems.at[q])

        for q in range(len(copies)):
            load(q).start()
        for q in range(len(copies)):
            load(q).wait()
            store(q).start()
        for q in range(len(copies)):
            store(q).wait()

    size = 2 * sum(int(np.prod(shape)) for shape in shapes)
    return pl.pallas_call(
        kernel,
        out_shape=[jax.ShapeDtypeStruct(shape, arrays[0].dtype) for shape in shapes],
        in_specs=[HBM] * len(arrays),
        out_specs=[HBM] * len(shapes),
        scratch_shapes=[pltpu.VMEM(shape, arrays[0].dtype) for _, _, shape, _, _ in copies]
        + [pltpu.SemaphoreType.DMA((len(copies),))] * 2,
        compiler_params=pltpu.CompilerParams(vmem_limit_bytes=VMEM),
        cost_estimate=pl.CostEstimate(flops=0, bytes_accessed=2 * size, transcendentals=0),
        name=name,
    )(*arrays)


def power_of(top):
    return jnp.floor(jnp.log2(jnp.maximum(top, 1e-30))) + 1.0


def code_tile(tile, power):
    return jnp.round(tile * (jnp.exp2(-power) * CODES)).astype(jnp.int32).astype(jnp.int16)


def top_of(tile):
    return jnp.max(jnp.abs(tile), axis=0, keepdims=True)


def gram_tiles(arrays, pieces, pairs, count, apart):
    rows = arrays[0].shape[-2]
    per, join = 4, 2
    deep = per * join * rows
    total = len(pieces) * per * rows
    slots = pairs.shape[0] // 2
    quarter = slots // 4
    strip = 256
    outs = [1, 1, 1, 1] if apart else [4]

    def kernel(pairs_ref, count_ref, *refs):
        array_refs, out_refs, (held, gram, made, powers, sems, out_sems) = refs[: len(arrays)], refs[len(arrays) : -6], refs[-6:]
        own = lax.axis_index("y") if apart else 0

        def load(p):
            a, i = pieces[p]
            return pltpu.make_async_copy(array_refs[a].at[i], held.at[pl.ds(p * per, per)], sems.at[p])

        def store(t):
            return pltpu.make_async_copy(made.at[t], out_refs[t].at[0] if apart else out_refs[0].at[t], out_sems.at[t])

        for p in range(len(pieces)):
            load(p).start()
        for p in range(0, len(pieces), join):
            for q in range(p, p + join):
                load(q).wait()
            units = pl.ds(p * per, per * join)

            for m in range(0, WIDTH, strip):
                part = lax.dot_general(
                    held[units, :, m : m + strip].reshape(deep, strip), held[units].reshape(deep, WIDTH),
                    (((0,), (0,)), ((), ())), preferred_element_type=jnp.float32,
                )
                if p == 0:
                    gram[m : m + strip, :] = part
                else:
                    gram[m : m + strip, :] += part

        for t in range(4):

            def tile_of(k, t=t):
                slot = (own + t) % 4 * quarter + k
                row = pl.multiple_of(pairs_ref[2 * slot] * BLOCK, BLOCK)
                col = pl.multiple_of(pairs_ref[2 * slot + 1] * BLOCK, BLOCK)
                return jnp.where(slot < count_ref[0], gram[pl.ds(row, BLOCK), pl.ds(col, BLOCK)], 0.0)

            def measure(k, carry, tile_of=tile_of):
                powers[pl.ds(k, 1), :] = top_of(tile_of(k))
                return carry

            def code(k, carry, t=t, tile_of=tile_of):
                span = pl.ds(pl.multiple_of(k * BLOCK, BLOCK), BLOCK)
                made[t, span, :] = code_tile(tile_of(k), powers[pl.ds(k, 1), :])
                return carry

            lax.fori_loop(0, quarter, measure, 0, unroll=4)
            powers[...] = power_of(powers[...])
            lax.fori_loop(0, quarter, code, 0, unroll=2)
            made[t, quarter * BLOCK :, :] = powers[...].astype(jnp.int32).astype(jnp.int16)
            store(t).start()
        for t in range(4):
            store(t).wait()

    return pl.pallas_call(
        kernel,
        out_shape=[jax.ShapeDtypeStruct((n, quarter * BLOCK + quarter, BLOCK), jnp.int16) for n in outs],
        grid_spec=pltpu.PrefetchScalarGridSpec(
            num_scalar_prefetch=2,
            grid=(),
            in_specs=[HBM] * len(arrays),
            out_specs=[HBM] * len(outs),
            scratch_shapes=[
                pltpu.VMEM((len(pieces) * per, rows, WIDTH), jnp.bfloat16),
                pltpu.VMEM((WIDTH, WIDTH), jnp.float32),
                pltpu.VMEM((4, quarter * BLOCK + quarter, BLOCK), jnp.int16),
                pltpu.VMEM((quarter, BLOCK), jnp.float32),
                pltpu.SemaphoreType.DMA((len(pieces),)),
                pltpu.SemaphoreType.DMA((4,)),
            ],
        ),
        compiler_params=pltpu.CompilerParams(vmem_limit_bytes=VMEM),
        cost_estimate=pl.CostEstimate(
            flops=2 * total * WIDTH * WIDTH, bytes_accessed=2 * total * WIDTH + 2 * slots * BLOCK * BLOCK,
            transcendentals=0,
        ),
        name="gram_tiles",
    )(pairs, count, *arrays)


def sum_tiles(parts, coded):
    rows = parts[0].shape[1]
    tiles = rows // (BLOCK + 1)
    sources = [(a, q) for a, part in enumerate(parts) for q in range(part.shape[0])]
    last = len(sources) * tiles

    def kernel(*refs):
        part_refs, out_ref, powers, sums = refs[: len(parts)], refs[len(parts)], refs[-2], refs[-1]
        for at, (a, q) in enumerate(sources):
            power = part_refs[a][q, tiles * BLOCK :, :].astype(jnp.int32).astype(jnp.float32)
            powers[at * tiles : (at + 1) * tiles, :] = jnp.exp2(power) * (1.0 / CODES)

        def span_of(k):
            return pl.ds(pl.multiple_of(k * BLOCK, BLOCK), BLOCK)

        def one(k, carry):
            total = None
            for at, (a, q) in enumerate(sources):
                values = part_refs[a][q, span_of(k), :].astype(jnp.int32).astype(jnp.float32)
                term = values * powers[pl.ds(at * tiles + k, 1), :]
                total = term if total is None else total + term
            if coded:
                sums[span_of(k), :] = total
                powers[pl.ds(last + k, 1), :] = top_of(total)
            else:
                out_ref[k] = total
            return carry

        lax.fori_loop(0, tiles, one, 0, unroll=2)
        if coded:
            own = power_of(powers[last:, :])
            powers[last:, :] = own

            def code(k, carry):
                out_ref[0, span_of(k), :] = code_tile(sums[span_of(k), :], powers[pl.ds(last + k, 1), :])
                return carry

            lax.fori_loop(0, tiles, code, 0, unroll=2)
            out_ref[0, tiles * BLOCK :, :] = own.astype(jnp.int32).astype(jnp.int16)

    if coded:
        out = jax.ShapeDtypeStruct((1, rows, BLOCK), jnp.int16)
    else:
        out = jax.ShapeDtypeStruct((tiles, BLOCK, BLOCK), jnp.float32)
    vmem = pl.BlockSpec(memory_space=pltpu.VMEM)
    return pl.pallas_call(
        kernel,
        out_shape=out,
        in_specs=[vmem] * len(parts),
        out_specs=vmem,
        scratch_shapes=[
            pltpu.VMEM((last + tiles, BLOCK), jnp.float32),
            pltpu.VMEM((tiles * BLOCK if coded else 8, BLOCK), jnp.float32),
        ],
        compiler_params=pltpu.CompilerParams(vmem_limit_bytes=VMEM),
        cost_estimate=pl.CostEstimate(
            flops=4 * len(sources) * rows * BLOCK, bytes_accessed=2 * (len(sources) + 2) * rows * BLOCK,
            transcendentals=0,
        ),
        name="sum_tiles",
    )(*parts)


def body(jacobian, obs_weight, block_order, tile_pairs, tile_count):
    rows = jacobian.shape[0]
    planes, lines, cores, quarters = (lax.axis_size(name) for name in ("z", "x", "c", "y"))
    group = lines * cores
    weight = obs_weight.reshape(1, rows)

    dests = [(k % lines, k // lines) for k in range(group)]

    def far_units(steps):
        return [(a, c, (s - FAR) * (1 - 2 * c)) for a, c in dests for s in steps]

    def near_units(step, there):
        return [(a, c, step) for a, c in dests if c in there]

    def up(value, step):
        return lax.ppermute(value, "z", [(b, (b + step) % planes) for b in range(planes)])

    def away(value, step):
        moves = [(b * cores + c, (b + step * (1 - 2 * c)) % planes * cores + c) for b in range(planes) for c in range(cores)]
        return lax.ppermute(value, ("z", "c"), moves)

    def spread(value, axes):
        return lax.all_to_all(value, axes, split_axis=0, concat_axis=0, tiled=True)

    def after(value, *others):
        return lax.optimization_barrier((value, *others))[0]

    wanted = jnp.concatenate([tile_pairs.reshape(-1), tile_count])
    far_wanted = away(wanted, FAR)

    units = far_units(FAR_FIRST) + near_units(1, (0, 1)) + near_units(-1, (0, 1)) + near_units(2, (0,)) + near_units(-2, (1,))
    shapes = [(group, len(FAR_FIRST)), (group,), (group,), (lines,), (lines,)]
    far_first, *near_parts = scale_columns(units, block_order, jacobian, weight, shapes)
    weight = after(weight, far_first)
    near_parts = [up(part, step) for part, step in zip(near_parts, (1, -1, 2, -2))]
    units = far_units(FAR_THEN) + near_units(0, (0, 1))
    far_then, stay = scale_columns(units, block_order, jacobian, weight, [(group, len(FAR_THEN)), (group,)])

    unit = (rows, WIDTH)
    half = [pl.ds(0, lines), pl.ds(lines, lines)]

    def parted(far, steps):
        sent = [k for k, s in enumerate(steps) if s]
        sent = [(k, h) for k in sent for h in half]
        copies = [(0, (h, k), (lines, *unit), q, pl.ds(0, lines)) for q, (k, h) in enumerate(sent)]
        parts = copy_parts([far], [(lines, *unit)] * len(sent), copies, "part_far")
        return [away(part, steps[k] // abs(steps[k])) for part, (k, _) in zip(parts, sent)]

    far_first = spread(far_first, ("c", "x"))
    far_first = after(far_first, stay)
    far_parts = parted(far_first, FAR_FIRST)
    far_then = after(far_then, far_first, *near_parts, far_parts[0])
    far_then = spread(far_then, ("c", "x"))
    far_parts += parted(far_then, FAR_THEN)

    pieces = [(0, 0, 4, 0), (0, 4, 4, 0), (1, 0, 4, 1), (1, 4, 4, 1), (2, 0, 4, 2), (3, 4, 4, 2), (4, 0, 4, 3), (4, 4, 4, 3)]
    near_parts.append(stay)
    (near,) = copy_parts(
        near_parts,
        [(group, 4, *unit)],
        [
            (a, pl.ds(first if near_parts[a].shape[0] == group else 0, n), (n, *unit), 0, (pl.ds(first, n), slot))
            for a, first, n, slot in pieces
        ],
        "join_near",
    )
    near = after(near, far_then, *far_parts[:4], far_wanted)
    far_parts[:2] = [away(part, -1) for part in far_parts[:2]]
    near = spread(near, ("c", "x")).reshape(group * 4, *unit)

    far_pieces = [(q, pl.ds(0, lines)) for q in range(len(far_parts))]
    far_pieces += [(len(far_parts), (h, FAR_FIRST.index(0))) for h in half]
    far_tiles = list(gram_tiles([*far_parts, far_first], far_pieces, far_wanted[:-1], far_wanted[-1:], True))
    near = after(near, far_tiles[1])
    for k in range(1, quarters):
        far_tiles[k] = lax.ppermute(far_tiles[k], "y", [(b, (b + k) % quarters) for b in range(quarters)])
    far_sum = away(sum_tiles(far_tiles, True), -FAR)
    near_pieces = [(0, pl.ds(lines * q, lines)) for q in range(8)]
    (near_tiles,) = gram_tiles([near], near_pieces, wanted[:-1], wanted[-1:], False)
    near_tiles = after(near_tiles, *far_tiles[1:])
    return sum_tiles([spread(near_tiles, "y"), far_sum], False)


def solution(mesh):
    shape = (4, mesh.shape["obs"] // 8, 2, mesh.shape["tile"])
    chips = jax.sharding.Mesh(mesh.devices.reshape(shape), ("x", "z", "c", "y"))
    everywhere = ("x", "z", "c", "y")
    owner = ("x", "z", "c")
    return jax.shard_map(
        body,
        mesh=chips,
        in_specs=(P(everywhere, None), P(everywhere), P(), P(owner, None, None), P(owner)),
        out_specs=P(everywhere, None, None),
        check_vma=False,
    )
```
